32 devices in a mesh: space: 4 (over x, core), tile: 8 (over z, y).
Axes of the slice: x: 2, y: 2, z: 4, core: 2. Of those that a mesh axis runs over, the one named last changes fastest.
Arguments:
- atom_feat: bfloat16 [512, 128, 128], P(('space', 'tile')), may hold values from -6 to 6
- atom_pos: bfloat16 [512, 3, 128], P(('space', 'tile')), may hold values from 0 to 4
- atom_counts: int32 [512], P(('space', 'tile')), may hold values from 32 to 128
- atom_nbrs: int32 [512, 4], P(('space', 'tile')), may hold values from 0 to 511, as said below
- probe_pos: float32 [64, 3, 512], P(('space', 'tile')), may hold values from 0 to 4
- probe_target: float32 [64, 512], P(('space', 'tile')), may hold values from -6 to 6
- tile_blocks: int32 [64, 8], P(('space', 'tile')), may hold values from 0 to 511, as said below
- atom_filter: bfloat16 [128, 1024], replicated, may hold values from -0.5 to 0.5
- probe_filter: bfloat16 [128, 1024], replicated, may hold values from -0.5 to 0.5
- mix_weight: bfloat16 [128, 128], replicated, may hold values from -0.5 to 0.5
- readout: float32 [128], replicated, may hold values from -0.5 to 0.5
Outputs:
- density: float32 [64, 512], P(('space', 'tile'))
- atom_filter_grad: float32 [128, 1024], replicated
- probe_filter_grad: float32 [128, 1024], replicated
- mix_grad: float32 [128, 128], replicated
- readout_grad: float32 [128], replicated
The draws below stay inside these ranges and needn't reach their ends.
Inputs may be any that keep to these rules, and one draw needn't show every extreme that they name: `atom_nbrs`: block g lies on device g // 16 in the order space then tile. The 4 neighbours of a block lie on devices of the same tile index whose space index differs by at most one, cyclically: the first one lower, the second one higher, the third the same; they need not be distinct. `tile_blocks`: the 8 blocks of a tile are distinct and lie on devices of the tile's own space index. The tiles of one device read at most 4 distinct blocks from any one device, and exactly 4 from some device.
All inputs are finite; a program needn't handle non-finite values.
Results may differ from the reference program's by a relative error of at most 0.0061.
Values may be sent and summed in bfloat16 or wider, within the bound.
A program may use at most 64 MiB of HBM per device.

```python
import jax
import jax.numpy as jnp
from jax import lax

C = 128
NRAD = 8
ABLK = 128
PT = 512
KB = 8
KA = 4
BLK_DEV = 16
TL_DEV = 2
RCAP = 4
BLOCKS = 512
TILES = 64
N_SPACE = 4
N_TILE = 8
DEVICES = 32


def draw_atom_nbrs(key, part):
    block_ids = jnp.arange(BLOCKS)
    space_of = block_ids // (N_TILE * BLK_DEV)
    tile_of = block_ids // BLK_DEV % N_TILE
    first_key, second_key = jax.random.split(jax.random.fold_in(key, 11))
    extra = jax.random.randint(first_key, (BLOCKS, KA - 3), -1, 2).astype(jnp.int32)
    shifts = jnp.concatenate([jnp.full((BLOCKS, 1), -1, jnp.int32), jnp.full((BLOCKS, 1), 1, jnp.int32), jnp.zeros((BLOCKS, 1), jnp.int32), extra], axis=1)
    within = jax.random.randint(second_key, (BLOCKS, KA), 0, BLK_DEV).astype(jnp.int32)
    target_space = (space_of[:, None] + shifts + N_SPACE) % N_SPACE
    return ((target_space * N_TILE + tile_of[:, None]) * BLK_DEV + within).astype(jnp.int32)


def draw_tile_blocks(key, part):
    slot_count = TL_DEV * KB
    unit_count = N_TILE * RCAP

    def one_device(device_key, device):
        split_keys = jax.random.split(device_key, 4)
        unit_peer = jnp.arange(unit_count) // RCAP
        favoured = jax.random.randint(split_keys[0], (), 0, N_TILE)
        priority = jax.random.randint(split_keys[1], (unit_count,), 0, 2 ** 20) * unit_count + jnp.arange(unit_count)
        priority = jnp.where(unit_peer == favoured, jnp.arange(unit_count) - unit_count, priority)
        picked = jnp.argsort(priority, stable=True)[:slot_count]
        peer_ids = unit_peer[picked]
        earlier = jnp.tril(jnp.ones((slot_count, slot_count), jnp.int32), -1)
        peer_rank = jnp.sum(earlier * (peer_ids[:, None] == peer_ids[None, :]).astype(jnp.int32), axis=1)
        orders = jax.vmap(lambda peer_key: jax.random.permutation(peer_key, BLK_DEV))(jax.random.split(split_keys[2], N_TILE))
        within = orders[peer_ids, peer_rank]
        region = device // N_TILE
        blocks = (region * N_TILE + peer_ids) * BLK_DEV + within
        shuffled = blocks[jax.random.permutation(split_keys[3], slot_count)]
        return shuffled.reshape(TL_DEV, KB)
    device_keys = jax.random.split(jax.random.fold_in(key, 23), DEVICES)
    return jax.vmap(one_device)(device_keys, jnp.arange(DEVICES)).reshape(TILES, KB).astype(jnp.int32)


def plant(entries, own_key, low, largest):
    shape = entries.shape
    spot = [jax.random.randint(jax.random.fold_in(own_key, axis), (), 0, shape[axis]) for axis in range(len(shape))]
    entries = entries.at[tuple(spot)].set(low)
    longest = shape.index(max(shape))
    spot[longest] = (spot[longest] + 1) % shape[longest]
    return entries.at[tuple(spot)].set(largest)


def level_of(own_key, extent, cuts, least, top_value):
    def one(dim, parts):
        steps = jax.random.uniform(jax.random.fold_in(jax.random.fold_in(own_key, 6), dim), (parts,), jnp.float32, least / len(cuts), top_value / len(cuts))
        return jnp.repeat(jnp.exp(steps), extent[dim] // parts).reshape((-1,) + (1,) * (len(extent) - dim - 1))

    level = one(*cuts[0])
    for cut in cuts[1:]:
        level = level * one(*cut)
    return level


def normal_values(stream_key, dims, deviation, reach, cuts=(), kind=jnp.bfloat16):
    entries = jax.random.normal(stream_key, dims, jnp.float32) * deviation
    if len(cuts) > 0:
        entries = level_of(stream_key, dims, cuts, -0.22, 0.18) * entries
    return jnp.clip(entries, min=-reach, max=reach).astype(kind)


def setup_inputs(seed: int = 0) -> dict:
    key_of = jax.random.split(jax.random.key(seed), 12)
    return {
        "atom_feat": normal_values(key_of[0], (BLOCKS, C, ABLK), 1.0, 6.0, ((0, 32),)),
        "atom_pos": jnp.clip(4.0 * jax.random.uniform(key_of[1], (BLOCKS, 3, ABLK), jnp.float32) ** level_of(key_of[1], (BLOCKS, 3, ABLK), ((0, 32),), -0.2, 0.2), 0.0, 4.0).astype(jnp.bfloat16),
        "atom_counts": plant(jax.random.randint(key_of[2], (BLOCKS,), ABLK // 4, ABLK + 1), jax.random.fold_in(key_of[2], 1), ABLK // 4, ABLK).astype(jnp.int32),
        "atom_nbrs": draw_atom_nbrs(jax.random.fold_in(key_of[11], 71), 0),
        "probe_pos": jnp.clip(4.0 * jax.random.uniform(key_of[4], (TILES, 3, PT), jnp.float32) ** level_of(key_of[4], (TILES, 3, PT), ((0, 32),), -0.2, 0.2), 0.0, 4.0),
        "probe_target": normal_values(key_of[5], (TILES, PT), 1.0, 6.0, ((0, 32),), jnp.float32),
        "tile_blocks": draw_tile_blocks(jax.random.fold_in(key_of[11], 71), 0),
        "atom_filter": normal_values(key_of[7], (C, NRAD * C), C ** -0.5, 0.5),
        "probe_filter": normal_values(key_of[8], (C, NRAD * C), C ** -0.5, 0.5),
        "mix_weight": normal_values(key_of[9], (C, C), C ** -0.5, 0.5),
        "readout": normal_values(key_of[10], (C,), C ** -0.5, 0.5, (), jnp.float32),
    }


CUTOFF = 6.0
SPACING = 0.75
SPREAD = 0.75

def silu_slope(values):
    sigmoid_part = jax.nn.sigmoid(values)
    return sigmoid_part * (1.0 + values * (1.0 - sigmoid_part))

def radial(source, target, factor):
    square = jnp.zeros((source.shape[1], target.shape[1]), source.dtype)
    for component in range(3):
        offset = source[component][:, None] - target[component][None, :]
        square = square + offset * offset
    distance = jnp.sqrt(square + 0.01)
    envelope = jnp.where(distance < CUTOFF, 0.5 * (jnp.cos(jnp.pi * distance / CUTOFF) + 1.0), 0.0)
    centers = jnp.arange(NRAD).astype(source.dtype) * SPACING
    shifted = (distance[None] - centers[:, None, None]) / SPREAD
    return jnp.exp(-shifted * shifted) * (envelope * factor)[None]

def rounded(values):
    narrow = lax.optimization_barrier(values.astype(jnp.bfloat16))
    return narrow.astype(jnp.float32)

def reference(atom_feat, atom_pos, atom_counts, atom_nbrs, probe_pos, probe_target, tile_blocks, atom_filter, probe_filter, mix_weight, readout):
    highest = lax.Precision.HIGHEST
    atom_mask = (jnp.arange(ABLK)[None, :] < atom_counts[:, None]).astype(jnp.float32)
    masked_feat = (atom_feat.astype(jnp.float32) * atom_mask[:, None, :]).astype(jnp.bfloat16)
    coords = atom_pos.astype(jnp.float32)
    atom_scale = (KA * ABLK) ** (-0.5)
    probe_scale = (KB * ABLK) ** (-0.5)

    def atom_block(block_index):
        sources = atom_nbrs[block_index]
        source_feat = masked_feat[sources].astype(jnp.float32)
        target_where = coords[block_index]
        kernel_rows = jax.vmap(lambda source: radial(source, target_where, atom_scale))(coords[sources])
        kernel_rows = rounded(kernel_rows)
        atom_sums = jnp.einsum('kcj,krji->rci', source_feat, kernel_rows)
        atom_sums = atom_sums.astype(jnp.bfloat16).reshape(NRAD * C, ABLK)
        message = jnp.dot(atom_filter, atom_sums, preferred_element_type=jnp.float32)
        updated = ((atom_feat[block_index].astype(jnp.float32) + jax.nn.silu(message)) * atom_mask[block_index][None, :]).astype(jnp.bfloat16)
        return (updated, atom_sums, message)
    updated, atom_sums, message = lax.map(atom_block, jnp.arange(BLOCKS))

    def probe_tile(tile_index):
        read_blocks = tile_blocks[tile_index]
        probe_where = probe_pos[tile_index]

        def kernel_of(block_id):
            return rounded(radial(coords[block_id], probe_where, probe_scale))

        def forward(total_sum, block_id):
            block_term = jnp.einsum('ca,rap->rcp', updated[block_id].astype(jnp.float32), kernel_of(block_id))
            return (total_sum + block_term, None)
        summed, _ = lax.scan(forward, jnp.zeros((NRAD, C, PT), jnp.float32), read_blocks)
        summed = summed.astype(jnp.bfloat16).reshape(NRAD * C, PT)
        hidden = jnp.dot(probe_filter, summed, preferred_element_type=jnp.float32)
        squashed = jax.nn.silu(hidden).astype(jnp.bfloat16)
        mixed_rows = jnp.dot(mix_weight, squashed, preferred_element_type=jnp.float32)
        outer_act = jax.nn.silu(mixed_rows)
        density = jnp.dot(readout, outer_act, precision=highest)
        misfit = (density - probe_target[tile_index]) / PT
        grad_readout = jnp.dot(outer_act, misfit, precision=highest)
        grad_mixed = (readout[:, None] * misfit[None, :] * silu_slope(mixed_rows)).astype(jnp.bfloat16)
        grad_mix = jnp.dot(grad_mixed, squashed.T, preferred_element_type=jnp.float32)
        grad_squashed = jnp.dot(mix_weight.T, grad_mixed, preferred_element_type=jnp.float32)
        grad_hidden = (grad_squashed * silu_slope(hidden)).astype(jnp.bfloat16)
        grad_probe = jnp.dot(grad_hidden, summed.T, preferred_element_type=jnp.float32)
        grad_summed = jnp.dot(probe_filter.T, grad_hidden, preferred_element_type=jnp.float32)
        grad_summed = grad_summed.astype(jnp.bfloat16).astype(jnp.float32).reshape(NRAD, C, PT)

        def backward(block_id):
            return jnp.einsum('rcp,rap->ca', grad_summed, kernel_of(block_id))
        grad_blocks = lax.map(backward, read_blocks)
        return (density, grad_probe, grad_mix, grad_readout, grad_blocks)
    density, grad_probe, grad_mix, grad_readout, grad_blocks = lax.map(probe_tile, jnp.arange(TILES))
    group_count = TILES // TL_DEV
    group_slots = TL_DEV * KB
    group_ids = tile_blocks.reshape(group_count, group_slots)
    group_grads = grad_blocks.reshape(group_count, group_slots, C, ABLK)
    earlier = jnp.tril(jnp.ones((group_slots, group_slots), jnp.float32), -1)

    def group_partial(pair):
        ids_here, grads_here = pair
        same = (ids_here[:, None] == ids_here[None, :]).astype(jnp.float32)
        summed = jnp.einsum('st,tca->sca', same, grads_here, precision=highest)
        repeated = lax.optimization_barrier(jnp.sum(earlier * same, axis=1)) > 0.5
        keep = jnp.where(repeated, 0.0, 1.0).astype(jnp.float32)
        return rounded(summed) * keep[:, None, None]
    partials = lax.map(group_partial, (group_ids, group_grads))
    block_grad = jnp.zeros((BLOCKS, C, ABLK), jnp.float32)
    block_grad = block_grad.at[tile_blocks.reshape(-1)].add(partials.reshape(TILES * KB, C, ABLK))
    grad_message = (block_grad * atom_mask[:, None, :] * silu_slope(message)).astype(jnp.bfloat16)
    atom_filter_grad = jnp.einsum('bca,bda->cd', grad_message.astype(jnp.float32), atom_sums.astype(jnp.float32))
    return (density, atom_filter_grad, lax.optimization_barrier(jnp.sum(grad_probe, axis=0)), lax.optimization_barrier(jnp.sum(grad_mix, axis=0)), lax.optimization_barrier(jnp.sum(grad_readout, axis=0)))
```

```python
import functools
import math

import jax
import jax.numpy as jnp
from jax import lax
from jax.experimental import pallas as pl
from jax.experimental.pallas import tpu as pltpu
from jax.sharding import PartitionSpec as P

CUTOFF = 6.0
SPACING = 0.75
SPREAD = 0.75
LOG2E = 1.4426950408889634
MESH = pl.DeviceIdType.MESH
VMEM_LIMIT = 56 * 1024 * 1024
F32 = jnp.float32
BF16 = jnp.bfloat16


def silu_slope(values):
    s = jax.nn.sigmoid(values)
    return s * (1.0 + values * (1.0 - s))


def radial(source_cols, target_rows, factor, filters):
    square = None
    for source, target in zip(source_cols, target_rows):
        offset = source - target
        square = offset * offset if square is None else square + offset * offset
    square = square + 0.01
    distance = square * lax.rsqrt(square)
    half = (math.pi / (2.0 * CUTOFF)) ** 2
    terms = [math.sqrt(factor) * (-half) ** k / math.factorial(2 * k) for k in range(7)]
    wave = terms[6] * square + terms[5]
    for term in terms[4::-1]:
        wave = wave * square + term
    envelope = jnp.where(square < CUTOFF * CUTOFF, wave * wave, 0.0)
    middle = filters // 2
    shifted = distance * (1.0 / SPREAD) - middle * (SPACING / SPREAD)
    step = SPACING / SPREAD
    centre = envelope * jnp.exp2(shifted * shifted * (-LOG2E))
    ratio = 2.0 * step * LOG2E
    up = jnp.exp2(shifted * ratio - step * step * LOG2E)
    down = jnp.exp2(shifted * (-ratio) - step * step * LOG2E)
    values = [None] * filters
    values[middle] = centre
    now = centre
    for k in range(filters - 1 - middle):
        now = now * (up if k == 0 else up * math.exp(-2.0 * k * step * step))
        values[middle + k + 1] = now
    now = centre
    for k in range(middle):
        now = now * (down if k == 0 else down * math.exp(-2.0 * k * step * step))
        values[middle - k - 1] = now
    return values


def dot(a, b):
    return jnp.dot(a, b, preferred_element_type=F32)


def dot_nt(a, b):
    return lax.dot_general(a, b, (((1,), (1,)), ((), ())), preferred_element_type=F32)


def atom_kernel(
    rows_ref, around_ref, where_ref, own_feat_ref, own_where_ref, filter_ref,
    stored_ref, sums_ref, message_ref, columns, radial_rows, feats,
):
    block = pl.program_id(0)
    channels, width = own_feat_ref.shape[1:]
    filters = filter_ref.shape[1] // channels
    nbrs = feats.shape[1] // width
    factor = (nbrs * width) ** (-0.5)
    own = own_where_ref[0].astype(F32)
    target = [own[c : c + 1, :] for c in range(3)]
    for k in range(nbrs):
        row = rows_ref[block * nbrs + k]
        where = where_ref[row].astype(F32)
        columns[k * width : (k + 1) * width, :] = where[:8].T
        keep = jnp.broadcast_to(where[3:4, :], (channels, width)) > 0.5
        feats[:, k * width : (k + 1) * width] = jnp.where(
            keep, around_ref[row].astype(F32), 0.0
        ).astype(BF16)
    chunk = 32

    def fill(step, carry):
        start = pl.multiple_of(step * chunk, chunk)
        source = [columns[pl.ds(start, chunk), c : c + 1] for c in range(3)]
        for r, value in enumerate(radial(source, target, factor, filters)):
            radial_rows[pl.ds(start, chunk), r * width : (r + 1) * width] = value.astype(BF16)
        return carry

    lax.fori_loop(0, nbrs * width // chunk, fill, 0, unroll=2)
    total = dot(feats[...], radial_rows[...]).astype(BF16)
    for r in range(filters):
        sums_ref[0, r * channels : (r + 1) * channels, :] = total[:, r * width : (r + 1) * width]
    message = dot(filter_ref[...], sums_ref[0])
    message_ref[0] = message
    updated = (own_feat_ref[0].astype(F32) + message * jax.nn.sigmoid(message)) * own[3:4, :]
    stored_ref[0, :channels, :] = updated.astype(BF16)
    stored_ref[0, channels:, :] = own_where_ref[0]


def probe_kernel(
    slots_ref, replies_ref, where_ref, target_ref, filter_ref, mix_ref, readout_ref,
    density_ref, grad_filter_ref, grad_mix_ref, grad_readout_ref, slot_grad_ref,
    columns, radial_rows, feats, summed, turned, slot_total,
):
    tile = pl.program_id(0)
    tiles = pl.num_programs(0)
    channels = mix_ref.shape[0]
    filters = filter_ref.shape[1] // channels
    width = replies_ref.shape[2]
    reads = feats.shape[1] // width
    probes = where_ref.shape[2]
    factor = (reads * width) ** (-0.5)

    @pl.when(tile == 0)
    def _():
        slot_total[...] = jnp.zeros_like(slot_total)
        grad_filter_ref[...] = jnp.zeros_like(grad_filter_ref)
        grad_mix_ref[...] = jnp.zeros_like(grad_mix_ref)
        grad_readout_ref[...] = jnp.zeros_like(grad_readout_ref)

    for k in range(reads):
        slot = slots_ref[tile * reads + k]
        row = replies_ref[slot]
        columns[k * width : (k + 1) * width, :] = row[channels:].astype(F32)[:8].T
        feats[:, k * width : (k + 1) * width] = row[:channels]
    chunk, span = 16, 256
    lanes = []
    for p in range(0, probes, span):
        lanes.append([where_ref[0, c : c + 1, p : p + span] for c in range(3)])

    def fill(step, carry):
        start = pl.multiple_of(step * chunk, chunk)
        source = [columns[pl.ds(start, chunk), c : c + 1] for c in range(3)]
        for n, target in enumerate(lanes):
            for r, value in enumerate(radial(source, target, factor, filters)):
                low = r * probes + n * span
                radial_rows[pl.ds(start, chunk), low : low + span] = value.astype(BF16)
        return carry

    lax.fori_loop(0, reads * width // chunk, fill, 0)
    for r in range(filters):
        summed[r * channels : (r + 1) * channels, :] = dot(
            feats[...], radial_rows[:, r * probes : (r + 1) * probes]
        ).astype(BF16)
    hidden = dot(filter_ref[...], summed[...])
    gate = jax.nn.sigmoid(hidden)
    squashed = (hidden * gate).astype(BF16)
    mixed = dot(mix_ref[...], squashed)
    mixed_gate = jax.nn.sigmoid(mixed)
    outer = mixed * mixed_gate
    readout = jnp.broadcast_to(readout_ref[...], (8, channels)).T[:, :1]
    density = jnp.sum(readout * outer, axis=0, keepdims=True)
    density_ref[0] = density
    misfit = (density - target_ref[0]) / probes
    part = jnp.sum(outer * misfit, axis=1, keepdims=True)
    grad_readout_ref[...] += jnp.broadcast_to(part, (channels, channels)).T[:8, :]
    grad_mixed = (
        readout * misfit * (mixed_gate * (1.0 + mixed * (1.0 - mixed_gate)))
    ).astype(BF16)
    grad_mix_ref[...] += dot_nt(grad_mixed, squashed)
    grad_squashed = dot(mix_ref[...].T, grad_mixed)
    grad_hidden = (grad_squashed * (gate * (1.0 + hidden * (1.0 - gate)))).astype(BF16)
    grad_filter_ref[...] += dot_nt(grad_hidden, summed[...])
    grad_sums = dot(grad_hidden.T, filter_ref[...]).astype(BF16)
    for r in range(filters):
        turned[r * probes : (r + 1) * probes, :] = grad_sums[:, r * channels : (r + 1) * channels]
    for k in range(reads):
        slot = slots_ref[tile * reads + k]
        back = dot(radial_rows[k * width : (k + 1) * width, :], turned[...])
        slot_total[slot] += back.T

    @pl.when(tile == tiles - 1)
    def _():
        slot_grad_ref[...] = slot_total[...].astype(BF16)


def final_kernel(ids_ref, returned_ref, where_ref, message_ref, sums_ref, grad_ref, totals):
    block = pl.program_id(0)

    @pl.when(block == 0)
    def _():
        totals[...] = jnp.zeros_like(totals)
        grad_ref[...] = jnp.zeros_like(grad_ref)

        def add(slot, carry):
            totals[ids_ref[slot]] += returned_ref[slot].astype(F32)
            return carry

        lax.fori_loop(0, returned_ref.shape[0], add, 0)

    keep = where_ref[0].astype(F32)[3:4, :]
    grad_message = (totals[block] * keep * silu_slope(message_ref[0])).astype(BF16)
    grad_ref[...] += dot_nt(grad_message, sums_ref[0])


def reduce_kernel(
    axes, atom_ref, filter_ref, mix_ref, readout_ref,
    atom_out, filter_out, mix_out, readout_out,
    total, sending, landing, gathered, send_sems, recv_sems,
):
    channels = atom_ref.shape[0]
    filters = atom_ref.shape[1] // channels
    rows = total.shape[0]
    partners = []
    for axis, size in axes:
        here = lax.axis_index(axis)
        bit = 1
        while bit < size:
            side = (here // bit) % 2
            partners.append((axis, here + bit * (1 - 2 * side), side))
            bit *= 2
    barrier = pltpu.get_barrier_semaphore()
    for axis, other, _ in partners:
        pl.semaphore_signal(barrier, inc=1, device_id={axis: other}, device_id_type=MESH)
    for r in range(filters):
        total[r * channels : (r + 1) * channels, :] = atom_ref[:, r * channels : (r + 1) * channels]
        low = (filters + r) * channels
        total[low : low + channels, :] = filter_ref[:, r * channels : (r + 1) * channels]
    low = 2 * filters * channels
    total[low : low + channels, :] = mix_ref[...]
    total[low + channels : low + channels + 8, :] = readout_ref[...]
    total[low + channels + 8 :, :] = jnp.zeros((rows - low - channels - 8, channels), F32)
    pl.semaphore_wait(barrier, len(partners))
    start = 0
    size = rows
    place = 0
    copies = []
    ranges = []
    for n, (axis, other, side) in enumerate(partners):
        size //= 2
        keep = pl.multiple_of(start + side * size, 16)
        give = pl.multiple_of(start + (1 - side) * size, 16)
        sending[place : place + size, :] = total[pl.ds(give, size), :].astype(BF16)
        copy = pltpu.make_async_remote_copy(
            src_ref=sending.at[pl.ds(place, size)],
            dst_ref=landing.at[pl.ds(place, size)],
            send_sem=send_sems.at[n],
            recv_sem=recv_sems.at[n],
            device_id={axis: other},
            device_id_type=MESH,
        )
        copy.start()
        copy.wait_recv()
        total[pl.ds(keep, size), :] += landing[place : place + size, :].astype(F32)
        copies.append(copy)
        ranges.append((keep, size))
        place += size
        start = keep
    keep, size = ranges[-1]
    gathered[pl.ds(keep, size), :] = total[pl.ds(keep, size), :].astype(BF16)
    for n in range(len(partners) - 1, -1, -1):
        axis, other, _ = partners[n]
        keep, size = ranges[n]
        copy = pltpu.make_async_remote_copy(
            src_ref=gathered.at[pl.ds(keep, size)],
            dst_ref=gathered.at[pl.ds(keep, size)],
            send_sem=send_sems.at[len(partners) + n],
            recv_sem=recv_sems.at[len(partners) + n],
            device_id={axis: other},
            device_id_type=MESH,
        )
        copy.start()
        copy.wait_recv()
        copies.append(copy)
    for r in range(filters):
        atom_out[:, r * channels : (r + 1) * channels] = gathered[
            r * channels : (r + 1) * channels, :
        ].astype(F32)
        low = (filters + r) * channels
        filter_out[:, r * channels : (r + 1) * channels] = gathered[low : low + channels, :].astype(F32)
    low = 2 * filters * channels
    mix_out[...] = gathered[low : low + channels, :].astype(F32)
    readout_out[...] = gathered[low + channels : low + channels + 16, :].astype(F32)[:8, :]
    for copy in copies:
        copy.wait_send()


def whole(array):
    return pl.BlockSpec(array.shape, lambda *_: (0,) * array.ndim)


def body(
    atom_feat, atom_pos, atom_counts, atom_nbrs, probe_pos, probe_target, tile_blocks,
    atom_filter, probe_filter, mix_weight, readout,
):
    blocks, channels, width = atom_feat.shape
    tiles, reads = tile_blocks.shape
    probes = probe_pos.shape[2]
    filters = atom_filter.shape[1] // channels
    nbrs = atom_nbrs.shape[1]
    peers = lax.axis_size("tile")
    space_count = lax.axis_size("space")
    here = lax.axis_index("space")
    params = pltpu.CompilerParams(vmem_limit_bytes=VMEM_LIMIT)
    mask = (jnp.arange(width)[None, :] < atom_counts[:, None]).astype(BF16)
    where = jnp.concatenate(
        [atom_pos, mask[:, None, :], jnp.zeros((blocks, 12, width), BF16)], axis=1
    )
    forward = [(i, (i + 1) % space_count) for i in range(space_count)]
    backward = [(b, a) for a, b in forward]
    around_feat = jnp.concatenate(
        [
            lax.ppermute(atom_feat, "space", forward),
            atom_feat,
            lax.ppermute(atom_feat, "space", backward),
        ],
        axis=0,
    )
    around_where = jnp.concatenate(
        [
            lax.ppermute(where, "space", forward),
            where,
            lax.ppermute(where, "space", backward),
        ],
        axis=0,
    )
    side = (atom_nbrs // (peers * blocks) - here + 1) % space_count
    source_rows = (side * blocks + atom_nbrs % blocks).reshape(-1)

    flat_owner = (tile_blocks // blocks % peers).reshape(-1)
    flat_spot = (tile_blocks % blocks).reshape(-1)
    cap = max(2, 2 * reads * tiles // peers)
    matches = (flat_owner[:, None, None] == jnp.arange(peers)[None, :, None]) & (
        flat_spot[:, None, None] == jnp.arange(blocks)[None, None, :]
    )
    needed = jnp.any(matches, axis=0).astype(jnp.int32)
    rank = jnp.cumsum(needed, axis=1) - needed
    chosen = (needed[:, None, :] == 1) & (rank[:, None, :] == jnp.arange(cap)[None, :, None])
    request_ids = jnp.sum(chosen.astype(jnp.int32) * jnp.arange(blocks)[None, None, :], axis=2)
    asked_ids = lax.all_to_all(request_ids, "tile", split_axis=0, concat_axis=0, tiled=True)
    picked_rank = jnp.sum(jnp.where(matches, rank[None], 0), axis=(1, 2))
    slot_index = flat_owner * cap + picked_rank
    slots = peers * cap

    rows = channels + 16
    one = lambda b, *_: (b, 0, 0)
    stored, sums, message = pl.pallas_call(
        atom_kernel,
        grid_spec=pltpu.PrefetchScalarGridSpec(
            num_scalar_prefetch=1,
            grid=(blocks,),
            in_specs=[
                whole(around_feat),
                whole(around_where),
                pl.BlockSpec((1, channels, width), one),
                pl.BlockSpec((1, 16, width), one),
                whole(atom_filter),
            ],
            out_specs=[
                pl.BlockSpec((1, rows, width), one),
                pl.BlockSpec((1, filters * channels, width), one),
                pl.BlockSpec((1, channels, width), one),
            ],
            scratch_shapes=[
                pltpu.VMEM((nbrs * width, 8), F32),
                pltpu.VMEM((nbrs * width, filters * width), BF16),
                pltpu.VMEM((channels, nbrs * width), BF16),
            ],
        ),
        out_shape=[
            jax.ShapeDtypeStruct((blocks, rows, width), BF16),
            jax.ShapeDtypeStruct((blocks, filters * channels, width), BF16),
            jax.ShapeDtypeStruct((blocks, channels, width), F32),
        ],
        compiler_params=params,
        name="atom_layer",
    )(source_rows, around_feat, around_where, atom_feat, where, atom_filter)

    sent = jnp.take(stored, asked_ids.reshape(-1), axis=0).reshape(peers, cap, rows, width)
    replies = lax.all_to_all(sent, "tile", split_axis=0, concat_axis=0, tiled=True)
    replies = replies.reshape(slots, rows, width)

    readout_row = readout.reshape(1, channels)
    density, grad_filter, grad_mix, grad_readout, slot_grad = pl.pallas_call(
        probe_kernel,
        grid_spec=pltpu.PrefetchScalarGridSpec(
            num_scalar_prefetch=1,
            grid=(tiles,),
            in_specs=[
                whole(replies),
                pl.BlockSpec((1, 3, probes), one),
                pl.BlockSpec((1, 1, probes), one),
                whole(probe_filter),
                whole(mix_weight),
                whole(readout_row),
            ],
            out_specs=[
                pl.BlockSpec((1, 1, probes), one),
                pl.BlockSpec((channels, filters * channels), lambda *_: (0, 0)),
                pl.BlockSpec((channels, channels), lambda *_: (0, 0)),
                pl.BlockSpec((8, channels), lambda *_: (0, 0)),
                pl.BlockSpec((slots, channels, width), lambda *_: (0, 0, 0)),
            ],
            scratch_shapes=[
                pltpu.VMEM((reads * width, 8), F32),
                pltpu.VMEM((reads * width, filters * probes), BF16),
                pltpu.VMEM((channels, reads * width), BF16),
                pltpu.VMEM((filters * channels, probes), BF16),
                pltpu.VMEM((filters * probes, channels), BF16),
                pltpu.VMEM((slots, channels, width), F32),
            ],
        ),
        out_shape=[
            jax.ShapeDtypeStruct((tiles, 1, probes), F32),
            jax.ShapeDtypeStruct((channels, filters * channels), F32),
            jax.ShapeDtypeStruct((channels, channels), F32),
            jax.ShapeDtypeStruct((8, channels), F32),
            jax.ShapeDtypeStruct((slots, channels, width), BF16),
        ],
        compiler_params=params,
        name="probe_layer",
    )(
        slot_index, replies, probe_pos, probe_target.reshape(tiles, 1, probes),
        probe_filter, mix_weight, readout_row,
    )

    returned = lax.all_to_all(
        slot_grad.reshape(peers, cap, channels, width), "tile",
        split_axis=0, concat_axis=0, tiled=True,
    ).reshape(slots, channels, width)
    grad_atom = pl.pallas_call(
        final_kernel,
        grid_spec=pltpu.PrefetchScalarGridSpec(
            num_scalar_prefetch=1,
            grid=(blocks,),
            in_specs=[
                whole(returned),
                pl.BlockSpec((1, 16, width), one),
                pl.BlockSpec((1, channels, width), one),
                pl.BlockSpec((1, filters * channels, width), one),
            ],
            out_specs=pl.BlockSpec((channels, filters * channels), lambda *_: (0, 0)),
            scratch_shapes=[pltpu.VMEM((blocks, channels, width), F32)],
        ),
        out_shape=jax.ShapeDtypeStruct((channels, filters * channels), F32),
        compiler_params=params,
        name="atom_grad",
    )(asked_ids.reshape(-1), returned, where, message, sums)

    axes = (("space", space_count), ("tile", peers))
    devices = space_count * peers
    real = 2 * filters * channels + channels + 16
    total_rows = -(-real // (16 * devices)) * 16 * devices
    steps = (devices - 1).bit_length()
    grads = (grad_atom, grad_filter, grad_mix, grad_readout)
    vmem = pl.BlockSpec(memory_space=pltpu.VMEM)
    grad_atom, grad_filter, grad_mix, grad_readout = pl.pallas_call(
        functools.partial(reduce_kernel, axes),
        in_specs=[vmem] * 4,
        out_specs=[vmem] * 4,
        out_shape=[jax.ShapeDtypeStruct(g.shape, F32) for g in grads],
        scratch_shapes=[
            pltpu.VMEM((total_rows, channels), F32),
            pltpu.VMEM((total_rows, channels), BF16),
            pltpu.VMEM((total_rows, channels), BF16),
            pltpu.VMEM((total_rows, channels), BF16),
            pltpu.SemaphoreType.DMA((2 * steps,)),
            pltpu.SemaphoreType.DMA((2 * steps,)),
        ],
        compiler_params=pltpu.CompilerParams(
            vmem_limit_bytes=VMEM_LIMIT, collective_id=0, has_side_effects=True
        ),
        name="grad_reduce",
    )(*grads)
    return (density.reshape(tiles, probes), grad_atom, grad_filter, grad_mix, grad_readout[0])


def solution(mesh):
    return jax.shard_map(
        body,
        mesh=mesh,
        in_specs=(
            P(("space", "tile"), None, None),
            P(("space", "tile"), None, None),
            P(("space", "tile")),
            P(("space", "tile"), None),
            P(("space", "tile"), None, None),
            P(("space", "tile"), None),
            P(("space", "tile"), None),
            P(),
            P(),
            P(),
            P(),
        ),
        out_specs=(P(("space", "tile"), None), P(), P(), P(), P()),
        check_vma=False,
    )
```

```python
import functools
import math

import jax
import jax.numpy as jnp
from jax import lax
from jax.experimental import pallas as pl
from jax.experimental.pallas import tpu as pltpu
from jax.sharding import PartitionSpec as P

CUTOFF = 6.0
SPACING = 0.75
SPREAD = 0.75
LOG2E = 1.4426950408889634
MESH = pl.DeviceIdType.MESH
VMEM_LIMIT = 56 * 1024 * 1024
F32 = jnp.float32
BF16 = jnp.bfloat16


def silu_slope(values):
    s = jax.nn.sigmoid(values)
    return s * (1.0 + values * (1.0 - s))


def radial(source_cols, target_rows, factor, filters, keep=None):
    square = None
    for source, target in zip(source_cols, target_rows):
        offset = source - target
        square = offset * offset if square is None else square + offset * offset
    square = square + 0.01
    distance = square * lax.rsqrt(square)
    half = (math.pi / (2.0 * CUTOFF)) ** 2
    terms = [math.sqrt(factor) * (-half) ** k / math.factorial(2 * k) for k in range(7)]
    wave = terms[6] * square + terms[5]
    for term in terms[4::-1]:
        wave = wave * square + term
    envelope = jnp.where(square < CUTOFF * CUTOFF, wave * wave, 0.0)
    middle = filters // 2
    shifted = distance * (1.0 / SPREAD) - middle * (SPACING / SPREAD)
    step = SPACING / SPREAD
    centre = envelope * jnp.exp2(shifted * shifted * (-LOG2E))
    if keep is not None:
        centre = centre * keep
    ratio = 2.0 * step * LOG2E
    up = jnp.exp2(shifted * ratio - step * step * LOG2E)
    down = jnp.exp2(shifted * (-ratio) - step * step * LOG2E)
    values = [None] * filters
    values[middle] = centre
    now = centre
    for k in range(filters - 1 - middle):
        now = now * (up if k == 0 else up * math.exp(-2.0 * k * step * step))
        values[middle + k + 1] = now
    now = centre
    for k in range(middle):
        now = now * (down if k == 0 else down * math.exp(-2.0 * k * step * step))
        values[middle - k - 1] = now
    return values


def dot(a, b):
    return jnp.dot(a, b, preferred_element_type=F32)


def dot_nt(a, b):
    return lax.dot_general(a, b, (((1,), (1,)), ((), ())), preferred_element_type=F32)


def atom_radial_kernel(rows_ref, around_where_ref, own_where_ref, radial_ref, columns):
    block = pl.program_id(0)
    width = own_where_ref.shape[2]
    nbrs = radial_ref.shape[1] // width
    filters = radial_ref.shape[2] // width
    factor = (nbrs * width) ** (-0.5)
    own = own_where_ref[0].astype(F32)
    target = [own[c : c + 1, :] for c in range(3)]
    for k in range(nbrs):
        where = around_where_ref[rows_ref[block * nbrs + k]].astype(F32)
        columns[k * width : (k + 1) * width, :] = where[:8].T
    chunk = 32

    def fill(step, carry):
        start = pl.multiple_of(step * chunk, chunk)
        source = [columns[pl.ds(start, chunk), c : c + 1] for c in range(3)]
        keep = columns[pl.ds(start, chunk), 3:4]
        for r, value in enumerate(radial(source, target, factor, filters, keep)):
            radial_ref[0, pl.ds(start, chunk), r * width : (r + 1) * width] = value.astype(BF16)
        return carry

    lax.fori_loop(0, nbrs * width // chunk, fill, 0, unroll=2)


def atom_kernel(
    rows_ref, sides_ref, asked_ref, low_ref, own_ref, high_ref, radial_ref, where_ref, filter_ref,
    sent_ref, sums_ref, message_ref, feats, updated,
):
    block = pl.program_id(0)
    channels, width = own_ref.shape[1:]
    filters = filter_ref.shape[1] // channels
    nbrs = feats.shape[1] // width
    for k in range(nbrs):
        row = rows_ref[block * nbrs + k]
        part = (slice(None), slice(k * width, (k + 1) * width))
        if k < 3:
            feats[part] = (low_ref, high_ref, own_ref)[k][row]
            continue
        side = sides_ref[block * nbrs + k]
        for n, ref in enumerate((low_ref, own_ref, high_ref)):

            @pl.when(side == n)
            def _(ref=ref, row=row, part=part):
                feats[part] = ref[row]

    total = dot(feats[...], radial_ref[0]).astype(BF16)
    for r in range(filters):
        sums_ref[0, r * channels : (r + 1) * channels, :] = total[:, r * width : (r + 1) * width]
    message = dot(filter_ref[...], sums_ref[0])
    message_ref[0] = message
    keep = where_ref[0].astype(F32)[3:4, :]
    fresh = (own_ref[block].astype(F32) + message * jax.nn.sigmoid(message)) * keep
    updated[block] = fresh.astype(BF16)

    @pl.when(block == pl.num_programs(0) - 1)
    def _():
        def pick(slot, carry):
            sent_ref[slot] = updated[asked_ref[slot]]
            return carry

        lax.fori_loop(0, sent_ref.shape[0], pick, 0)


def probe_radial_kernel(source_ref, where_ref, radial_ref, columns):
    width = source_ref.shape[2]
    reads = source_ref.shape[0]
    probes = where_ref.shape[2]
    filters = radial_ref.shape[2] // probes
    factor = (pl.num_programs(1) * reads * width) ** (-0.5)
    for k in range(reads):
        columns[k * width : (k + 1) * width, :] = source_ref[k].T
    chunk, span = 16, 256
    lanes = []
    for p in range(0, probes, span):
        lanes.append([where_ref[0, c : c + 1, p : p + span] for c in range(3)])

    def fill(step, carry):
        start = pl.multiple_of(step * chunk, chunk)
        source = [columns[pl.ds(start, chunk), c : c + 1] for c in range(3)]
        for n, target in enumerate(lanes):
            for r, value in enumerate(radial(source, target, factor, filters)):
                low = r * probes + n * span
                radial_ref[0, pl.ds(start, chunk), low : low + span] = value.astype(BF16)
        return carry

    lax.fori_loop(0, reads * width // chunk, fill, 0)


def probe_kernel(
    slots_ref, replies_ref, radial_ref, target_ref, filter_ref, mix_ref, readout_ref,
    density_ref, grad_filter_ref, grad_mix_ref, grad_readout_ref, slot_grad_ref,
    feats, summed, turned, slot_total,
):
    tile = pl.program_id(0)
    tiles = pl.num_programs(0)
    channels = mix_ref.shape[0]
    filters = filter_ref.shape[1] // channels
    width = replies_ref.shape[2]
    reads = feats.shape[1] // width
    probes = target_ref.shape[2]

    @pl.when(tile == 0)
    def _():
        slot_total[...] = jnp.zeros_like(slot_total)
        grad_filter_ref[...] = jnp.zeros_like(grad_filter_ref)
        grad_mix_ref[...] = jnp.zeros_like(grad_mix_ref)
        grad_readout_ref[...] = jnp.zeros_like(grad_readout_ref)

    for k in range(reads):
        feats[:, k * width : (k + 1) * width] = replies_ref[slots_ref[tile * reads + k]]
    for r in range(filters):
        summed[r * channels : (r + 1) * channels, :] = dot(
            feats[...], radial_ref[0, :, r * probes : (r + 1) * probes]
        ).astype(BF16)
    hidden = dot(filter_ref[...], summed[...])
    gate = jax.nn.sigmoid(hidden)
    squashed = (hidden * gate).astype(BF16)
    mixed = dot(mix_ref[...], squashed)
    mixed_gate = jax.nn.sigmoid(mixed)
    outer = mixed * mixed_gate
    readout = jnp.broadcast_to(readout_ref[...], (8, channels)).T[:, :1]
    density = jnp.sum(readout * outer, axis=0, keepdims=True)
    density_ref[0] = density
    misfit = (density - target_ref[0]) / probes
    part = jnp.sum(outer * misfit, axis=1, keepdims=True)
    grad_readout_ref[...] += jnp.broadcast_to(part, (channels, channels)).T[:8, :]
    grad_mixed = (
        readout * misfit * (mixed_gate * (1.0 + mixed * (1.0 - mixed_gate)))
    ).astype(BF16)
    grad_mix_ref[...] += dot_nt(grad_mixed, squashed)
    grad_squashed = dot(mix_ref[...].T, grad_mixed)
    grad_hidden = (grad_squashed * (gate * (1.0 + hidden * (1.0 - gate)))).astype(BF16)
    grad_filter_ref[...] += dot_nt(grad_hidden, summed[...])
    grad_sums = dot(grad_hidden.T, filter_ref[...]).astype(BF16)
    for r in range(filters):
        turned[r * probes : (r + 1) * probes, :] = grad_sums[:, r * channels : (r + 1) * channels]
    for k in range(reads):
        slot = slots_ref[tile * reads + k]
        back = dot(radial_ref[0, k * width : (k + 1) * width, :], turned[...])
        slot_total[slot] += back.T

    @pl.when(tile == tiles - 1)
    def _():
        slot_grad_ref[...] = slot_total[...].astype(BF16)


def final_kernel(ids_ref, returned_ref, where_ref, message_ref, sums_ref, grad_ref, totals):
    step = pl.program_id(0)
    group = sums_ref.shape[0]

    @pl.when(step == 0)
    def _():
        totals[...] = jnp.zeros_like(totals)

        def add(slot, carry):
            totals[ids_ref[slot]] += returned_ref[slot].astype(F32)
            return carry

        lax.fori_loop(0, returned_ref.shape[0], add, 0)

    grads = []
    for n in range(group):
        keep = where_ref[n].astype(F32)[3:4, :]
        grad = totals[step * group + n] * keep * silu_slope(message_ref[n])
        grads.append(grad.astype(BF16))
    part = dot_nt(
        jnp.concatenate(grads, axis=1),
        jnp.concatenate([sums_ref[n] for n in range(group)], axis=1),
    )

    @pl.when(step == 0)
    def _():
        grad_ref[...] = part

    @pl.when(step > 0)
    def _():
        grad_ref[...] += part


def reduce_kernel(axes, count, *refs):
    ins, outs = refs[:count], refs[count : 2 * count]
    total, sending, landing, gathered, send_sems, recv_sems = refs[2 * count :]
    lanes = total.shape[1]
    rows = total.shape[0]
    partners = []
    for axis, size in axes:
        here = lax.axis_index(axis)
        bit = 1
        while bit < size:
            side = (here // bit) % 2
            partners.append((axis, here + bit * (1 - 2 * side), side))
            bit *= 2
    barrier = pltpu.get_barrier_semaphore()
    for axis, other, _ in partners:
        pl.semaphore_signal(barrier, inc=1, device_id={axis: other}, device_id_type=MESH)
    pieces = []
    low = 0
    for index, ref in enumerate(ins):
        height = ref.shape[0]
        for left in range(0, ref.shape[1], lanes):
            total[low : low + height, :] = ref[:, left : left + lanes]
            pieces.append((index, left, low, height))
            low += height
    if low < rows:
        total[low:, :] = jnp.zeros((rows - low, lanes), F32)
    pl.semaphore_wait(barrier, len(partners))
    start = 0
    size = rows
    place = 0
    copies = []
    ranges = []
    for n, (axis, other, side) in enumerate(partners):
        size //= 2
        keep = pl.multiple_of(start + side * size, 16)
        give = pl.multiple_of(start + (1 - side) * size, 16)
        sending[place : place + size, :] = total[pl.ds(give, size), :].astype(BF16)
        copy = pltpu.make_async_remote_copy(
            src_ref=sending.at[pl.ds(place, size)],
            dst_ref=landing.at[pl.ds(place, size)],
            send_sem=send_sems.at[n],
            recv_sem=recv_sems.at[n],
            device_id={axis: other},
            device_id_type=MESH,
        )
        copy.start()
        copy.wait_recv()
        total[pl.ds(keep, size), :] += landing[place : place + size, :].astype(F32)
        copies.append(copy)
        ranges.append((keep, size))
        place += size
        start = keep
    keep, size = ranges[-1]
    gathered[pl.ds(keep, size), :] = total[pl.ds(keep, size), :].astype(BF16)
    for n in range(len(partners) - 1, -1, -1):
        axis, other, _ = partners[n]
        keep, size = ranges[n]
        copy = pltpu.make_async_remote_copy(
            src_ref=gathered.at[pl.ds(keep, size)],
            dst_ref=gathered.at[pl.ds(keep, size)],
            send_sem=send_sems.at[len(partners) + n],
            recv_sem=recv_sems.at[len(partners) + n],
            device_id={axis: other},
            device_id_type=MESH,
        )
        copy.start()
        copy.wait_recv()
        copies.append(copy)
    for index, left, low, height in pieces:
        padded = -(-height // 16) * 16
        part = gathered[low : low + padded, :].astype(F32)[:height]
        outs[index][:, left : left + lanes] = part
    for copy in copies:
        copy.wait_send()


def reduce_all(grads, axes, name, collective_id):
    devices = math.prod(size for _, size in axes)
    lanes = grads[0].shape[0]
    real = sum(-(-g.size // (16 * lanes)) * 16 for g in grads)
    rows = -(-real // (16 * devices)) * 16 * devices
    steps = (devices - 1).bit_length()
    vmem = pl.BlockSpec(memory_space=pltpu.VMEM)
    return pl.pallas_call(
        functools.partial(reduce_kernel, axes, len(grads)),
        in_specs=[vmem] * len(grads),
        out_specs=[vmem] * len(grads),
        out_shape=[jax.ShapeDtypeStruct(g.shape, F32) for g in grads],
        scratch_shapes=[
            pltpu.VMEM((rows, lanes), F32),
            pltpu.VMEM((rows, lanes), BF16),
            pltpu.VMEM((rows, lanes), BF16),
            pltpu.VMEM((rows, lanes), BF16),
            pltpu.SemaphoreType.DMA((2 * steps,)),
            pltpu.SemaphoreType.DMA((2 * steps,)),
        ],
        compiler_params=pltpu.CompilerParams(
            vmem_limit_bytes=16 * 1024 * 1024, collective_id=collective_id, has_side_effects=True
        ),
        cost_estimate=cost(20e9),
        name=name,
    )(*grads)


def cost(flops):
    return pl.CostEstimate(flops=int(flops), bytes_accessed=1 << 20, transcendentals=0)


def whole(array):
    return pl.BlockSpec(array.shape, lambda *_: (0,) * array.ndim)


def body(
    atom_feat, atom_pos, atom_counts, atom_nbrs, probe_pos, probe_target, tile_blocks,
    atom_filter, probe_filter, mix_weight, readout,
):
    blocks, channels, width = atom_feat.shape
    tiles, reads = tile_blocks.shape
    probes = probe_pos.shape[2]
    filters = atom_filter.shape[1] // channels
    nbrs = atom_nbrs.shape[1]
    peers = lax.axis_size("tile")
    space_count = lax.axis_size("space")
    here = lax.axis_index("space")
    params = pltpu.CompilerParams(vmem_limit_bytes=VMEM_LIMIT)
    small = pltpu.CompilerParams(vmem_limit_bytes=16 * 1024 * 1024)
    mask = (jnp.arange(width)[None, :] < atom_counts[:, None]).astype(BF16)
    where = jnp.concatenate(
        [atom_pos, mask[:, None, :], jnp.zeros((blocks, 12, width), BF16)], axis=1
    )
    forward = [(i, (i + 1) % space_count) for i in range(space_count)]
    backward = [(b, a) for a, b in forward]
    low_feat = lax.ppermute(atom_feat, "space", forward)
    high_feat = lax.ppermute(atom_feat, "space", backward)
    around_where = jnp.concatenate(
        [lax.ppermute(where, "space", forward), where, lax.ppermute(where, "space", backward)],
        axis=0,
    )
    sides = ((atom_nbrs // (peers * blocks) - here + 1) % space_count).reshape(-1)
    near_rows = (atom_nbrs % blocks).reshape(-1)

    flat_owner = (tile_blocks // blocks % peers).reshape(-1)
    flat_spot = (tile_blocks % blocks).reshape(-1)
    cap = max(2, 2 * reads * tiles // peers)
    slots = peers * cap
    matches = (flat_owner[:, None, None] == jnp.arange(peers)[None, :, None]) & (
        flat_spot[:, None, None] == jnp.arange(blocks)[None, None, :]
    )
    needed = jnp.any(matches, axis=0).astype(jnp.int32)
    rank = jnp.cumsum(needed, axis=1) - needed
    chosen = (needed[:, None, :] == 1) & (rank[:, None, :] == jnp.arange(cap)[None, :, None])
    request_ids = jnp.sum(chosen.astype(jnp.int32) * jnp.arange(blocks)[None, None, :], axis=2)
    picked_rank = jnp.sum(jnp.where(matches, rank[None], 0), axis=(1, 2))
    slot_index = flat_owner * cap + picked_rank
    flat_where = jnp.broadcast_to(
        atom_pos.reshape(1, blocks * 3, width), (peers, blocks * 3, width)
    )
    asked_row = jnp.pad(request_ids.astype(BF16)[:, None, :], ((0, 0), (0, 15), (0, width - cap)))
    notes = lax.all_to_all(
        jnp.concatenate([flat_where, asked_row], axis=1), "tile",
        split_axis=0, concat_axis=0, tiled=True,
    )
    asked_ids = notes[:, blocks * 3, :cap].astype(jnp.int32).reshape(-1)
    group_where = notes[:, : blocks * 3, :].reshape(peers * blocks, 3, width)

    one = lambda b, *_: (b, 0, 0)
    atom_radial = pl.pallas_call(
        atom_radial_kernel,
        grid_spec=pltpu.PrefetchScalarGridSpec(
            num_scalar_prefetch=1,
            grid=(blocks,),
            in_specs=[whole(around_where), pl.BlockSpec((1, 16, width), one)],
            out_specs=pl.BlockSpec((1, nbrs * width, filters * width), one),
            scratch_shapes=[pltpu.VMEM((nbrs * width, 8), F32)],
        ),
        out_shape=jax.ShapeDtypeStruct((blocks, nbrs * width, filters * width), BF16),
        compiler_params=small,
        cost_estimate=cost(20e9),
        name="atom_radial",
    )(sides * blocks + near_rows, around_where, where)

    sent, sums, message = pl.pallas_call(
        atom_kernel,
        grid_spec=pltpu.PrefetchScalarGridSpec(
            num_scalar_prefetch=3,
            grid=(blocks,),
            in_specs=[
                whole(low_feat),
                whole(atom_feat),
                whole(high_feat),
                pl.BlockSpec((1, nbrs * width, filters * width), one),
                pl.BlockSpec((1, 16, width), one),
                whole(atom_filter),
            ],
            out_specs=[
                pl.BlockSpec((slots, channels, width), lambda *_: (0, 0, 0)),
                pl.BlockSpec((1, filters * channels, width), one),
                pl.BlockSpec((1, channels, width), one),
            ],
            scratch_shapes=[
                pltpu.VMEM((channels, nbrs * width), BF16),
                pltpu.VMEM((blocks, channels, width), BF16),
            ],
        ),
        out_shape=[
            jax.ShapeDtypeStruct((slots, channels, width), BF16),
            jax.ShapeDtypeStruct((blocks, filters * channels, width), BF16),
            jax.ShapeDtypeStruct((blocks, channels, width), F32),
        ],
        compiler_params=params,
        cost_estimate=cost(10e9),
        name="atom_layer",
    )(near_rows, sides, asked_ids, low_feat, atom_feat, high_feat, atom_radial, where, atom_filter)

    sent, group_where = lax.optimization_barrier((sent, group_where))
    replies = lax.all_to_all(
        sent.reshape(peers, cap, channels, width), "tile",
        split_axis=0, concat_axis=0, tiled=True,
    ).reshape(slots, channels, width)

    source_where = jnp.take(group_where, flat_owner * blocks + flat_spot, axis=0).astype(F32)
    source_where = jnp.pad(source_where, ((0, 0), (0, 5), (0, 0)))
    pieces = reads // 2
    per = reads // pieces
    probe_radial = pl.pallas_call(
        probe_radial_kernel,
        grid=(tiles, pieces),
        in_specs=[
            pl.BlockSpec((per, 8, width), lambda t, n: (t * pieces + n, 0, 0)),
            pl.BlockSpec((1, 3, probes), lambda t, n: (t, 0, 0)),
        ],
        out_specs=pl.BlockSpec((1, per * width, filters * probes), lambda t, n: (t, n, 0)),
        scratch_shapes=[pltpu.VMEM((per * width, 8), F32)],
        out_shape=jax.ShapeDtypeStruct((tiles, reads * width, filters * probes), BF16),
        compiler_params=small,
        cost_estimate=cost(20e9),
        name="probe_radial",
    )(source_where, probe_pos)

    readout_row = readout.reshape(1, channels)
    density, grad_filter, grad_mix, grad_readout, slot_grad = pl.pallas_call(
        probe_kernel,
        grid_spec=pltpu.PrefetchScalarGridSpec(
            num_scalar_prefetch=1,
            grid=(tiles,),
            in_specs=[
                whole(replies),
                pl.BlockSpec((1, reads * width, filters * probes), one),
                pl.BlockSpec((1, 1, probes), one),
                whole(probe_filter),
                whole(mix_weight),
                whole(readout_row),
            ],
            out_specs=[
                pl.BlockSpec((1, 1, probes), one),
                pl.BlockSpec((channels, filters * channels), lambda *_: (0, 0)),
                pl.BlockSpec((channels, channels), lambda *_: (0, 0)),
                pl.BlockSpec((8, channels), lambda *_: (0, 0)),
                pl.BlockSpec((slots, channels, width), lambda *_: (0, 0, 0)),
            ],
            scratch_shapes=[
                pltpu.VMEM((channels, reads * width), BF16),
                pltpu.VMEM((filters * channels, probes), BF16),
                pltpu.VMEM((filters * probes, channels), BF16),
                pltpu.VMEM((slots, channels, width), F32),
            ],
        ),
        out_shape=[
            jax.ShapeDtypeStruct((tiles, 1, probes), F32),
            jax.ShapeDtypeStruct((channels, filters * channels), F32),
            jax.ShapeDtypeStruct((channels, channels), F32),
            jax.ShapeDtypeStruct((8, channels), F32),
            jax.ShapeDtypeStruct((slots, channels, width), BF16),
        ],
        compiler_params=params,
        cost_estimate=cost(10e9),
        name="probe_layer",
    )(
        slot_index, replies, probe_radial, probe_target.reshape(tiles, 1, probes),
        probe_filter, mix_weight, readout_row,
    )

    returned = lax.all_to_all(
        slot_grad.reshape(peers, cap, channels, width), "tile",
        split_axis=0, concat_axis=0, tiled=True,
    ).reshape(slots, channels, width)
    axes = (("space", space_count), ("tile", peers))
    grad_filter, grad_mix, grad_readout = reduce_all(
        (grad_filter, grad_mix, grad_readout), axes, "probe_reduce", 0
    )
    group = math.gcd(blocks, 4)
    grad_atom = pl.pallas_call(
        final_kernel,
        grid_spec=pltpu.PrefetchScalarGridSpec(
            num_scalar_prefetch=1,
            grid=(blocks // group,),
            in_specs=[
                whole(returned),
                pl.BlockSpec((group, 16, width), one),
                pl.BlockSpec((group, channels, width), one),
                pl.BlockSpec((group, filters * channels, width), one),
            ],
            out_specs=pl.BlockSpec((channels, filters * channels), lambda *_: (0, 0)),
            scratch_shapes=[pltpu.VMEM((blocks, channels, width), F32)],
        ),
        out_shape=jax.ShapeDtypeStruct((channels, filters * channels), F32),
        compiler_params=params,
        cost_estimate=cost(10e9),
        name="atom_grad",
    )(asked_ids, returned, where, message, sums)
    (grad_atom,) = reduce_all((grad_atom,), axes, "atom_reduce", 1)
    return (density.reshape(tiles, probes), grad_atom, grad_filter, grad_mix, grad_readout[0])


def solution(mesh):
    return jax.shard_map(
        body,
        mesh=mesh,
        in_specs=(
            P(("space", "tile"), None, None),
            P(("space", "tile"), None, None),
            P(("space", "tile")),
            P(("space", "tile"), None),
            P(("space", "tile"), None, None),
            P(("space", "tile"), None),
            P(("space", "tile"), None),
            P(),
            P(),
            P(),
            P(),
        ),
        out_specs=(P(("space", "tile"), None), P(), P(), P(), P()),
        check_vma=False,
    )
```

```python
import functools
import math

import jax
import jax.numpy as jnp
from jax import lax
from jax.experimental import pallas as pl
from jax.experimental.pallas import tpu as pltpu
from jax.sharding import PartitionSpec as P

CUTOFF = 6.0
SPACING = 0.75
SPREAD = 0.75
LOG2E = 1.4426950408889634
MESH = pl.DeviceIdType.MESH
VMEM_LIMIT = 60 * 1024 * 1024
F32 = jnp.float32
BF16 = jnp.bfloat16


def silu_slope(values):
    s = jax.nn.sigmoid(values)
    return s * (1.0 + values * (1.0 - s))


def radial(source_cols, target_rows, factor, filters, keep=None):
    square = None
    for source, target in zip(source_cols, target_rows):
        offset = source - target
        square = offset * offset if square is None else square + offset * offset
    square = square + 0.01
    distance = square * lax.rsqrt(square)
    half = (math.pi / (2.0 * CUTOFF)) ** 2
    terms = [math.sqrt(factor) * (-half) ** k / math.factorial(2 * k) for k in range(7)]
    wave = terms[6] * square + terms[5]
    for term in terms[4::-1]:
        wave = wave * square + term
    envelope = jnp.where(square < CUTOFF * CUTOFF, wave * wave, 0.0)
    middle = filters // 2
    shifted = distance * (1.0 / SPREAD) - middle * (SPACING / SPREAD)
    step = SPACING / SPREAD
    centre = envelope * jnp.exp2(shifted * shifted * (-LOG2E))
    if keep is not None:
        centre = centre * keep
    ratio = 2.0 * step * LOG2E
    up = jnp.exp2(shifted * ratio)
    down = jnp.exp2(shifted * (-ratio))
    values = [None] * filters
    values[middle] = centre
    for r in range(middle + 1, filters):
        values[r] = values[r - 1] * up
    for r in range(middle - 1, -1, -1):
        values[r] = values[r + 1] * down
    return values


def filter_weight(r, filters):
    return math.exp(-(((r - filters // 2) * SPACING / SPREAD) ** 2))


def dot(a, b):
    return jnp.dot(a, b, preferred_element_type=F32)


def dot_nt(a, b):
    return lax.dot_general(a, b, (((1,), (1,)), ((), ())), preferred_element_type=F32)


def atom_radial_kernel(rows_ref, around_where_ref, own_where_ref, radial_ref, columns):
    block = pl.program_id(0)
    width = own_where_ref.shape[2]
    nbrs = radial_ref.shape[1] // width
    filters = radial_ref.shape[2] // width
    factor = (nbrs * width) ** (-0.5)
    own = own_where_ref[0].astype(F32)
    target = [own[c : c + 1, :] for c in range(3)]
    for k in range(nbrs):
        where = around_where_ref[rows_ref[block * nbrs + k]].astype(F32)
        columns[k * width : (k + 1) * width, :] = where[:8].T
    chunk = 32

    def fill(step, carry):
        start = pl.multiple_of(step * chunk, chunk)
        source = [columns[pl.ds(start, chunk), c : c + 1] for c in range(3)]
        keep = columns[pl.ds(start, chunk), 3:4]
        for r, value in enumerate(radial(source, target, factor, filters, keep)):
            radial_ref[0, pl.ds(start, chunk), r * width : (r + 1) * width] = value.astype(BF16)
        return carry

    lax.fori_loop(0, nbrs * width // chunk, fill, 0, unroll=2)


def atom_kernel(
    rows_ref, sides_ref, asked_ref, low_ref, own_ref, high_ref, radial_ref, where_ref, filter_ref,
    sent_ref, sums_ref, message_ref, feats, updated,
):
    block = pl.program_id(0)
    channels, width = own_ref.shape[1:]
    filters = filter_ref.shape[1] // channels
    nbrs = feats.shape[1] // width
    for k in range(nbrs):
        row = rows_ref[block * nbrs + k]
        part = (slice(None), slice(k * width, (k + 1) * width))
        if k < 3:
            feats[part] = (low_ref, high_ref, own_ref)[k][row]
            continue
        side = sides_ref[block * nbrs + k]
        for n, ref in enumerate((low_ref, own_ref, high_ref)):

            @pl.when(side == n)
            def _(ref=ref, row=row, part=part):
                feats[part] = ref[row]

    total = dot(feats[...], radial_ref[0])
    for r in range(filters):
        part = total[:, r * width : (r + 1) * width] * filter_weight(r, filters)
        sums_ref[0, r * channels : (r + 1) * channels, :] = part.astype(BF16)
    message = dot(filter_ref[...], sums_ref[0])
    message_ref[0] = message
    keep = where_ref[0].astype(F32)[3:4, :]
    fresh = (own_ref[block].astype(F32) + message * jax.nn.sigmoid(message)) * keep
    updated[block] = fresh.astype(BF16)

    @pl.when(block == pl.num_programs(0) - 1)
    def _():
        def pick(slot, carry):
            sent_ref[slot] = updated[asked_ref[slot]]
            return carry

        lax.fori_loop(0, sent_ref.shape[0], pick, 0)


def probe_radial_kernel(source_ref, where_ref, radial_ref, columns):
    width = source_ref.shape[2]
    reads = source_ref.shape[0]
    probes = where_ref.shape[2]
    filters = radial_ref.shape[2] // probes
    factor = (pl.num_programs(1) * reads * width) ** (-0.5)
    for k in range(reads):
        columns[k * width : (k + 1) * width, :] = source_ref[k].T
    chunk, span = 16, 256
    lanes = []
    for p in range(0, probes, span):
        lanes.append([where_ref[0, c : c + 1, p : p + span] for c in range(3)])

    def fill(step, carry):
        start = pl.multiple_of(step * chunk, chunk)
        source = [columns[pl.ds(start, chunk), c : c + 1] for c in range(3)]
        for n, target in enumerate(lanes):
            for r, value in enumerate(radial(source, target, factor, filters)):
                low = r * probes + n * span
                radial_ref[0, pl.ds(start, chunk), low : low + span] = value.astype(BF16)
        return carry

    lax.fori_loop(0, reads * width // chunk, fill, 0)


def probe_kernel(
    slots_ref, replies_ref, radial_ref, target_ref, filter_ref, mix_ref, readout_ref,
    density_ref, grad_filter_ref, grad_mix_ref, grad_readout_ref, slot_grad_ref,
    feats, summed, turned, slot_total,
):
    tile = pl.program_id(0)
    tiles = pl.num_programs(0)
    channels = mix_ref.shape[0]
    filters = filter_ref.shape[1] // channels
    width = replies_ref.shape[2]
    reads = feats.shape[1] // width
    probes = target_ref.shape[2]

    @pl.when(tile == 0)
    def _():
        slot_total[...] = jnp.zeros_like(slot_total)
        grad_filter_ref[...] = jnp.zeros_like(grad_filter_ref)
        grad_mix_ref[...] = jnp.zeros_like(grad_mix_ref)
        grad_readout_ref[...] = jnp.zeros_like(grad_readout_ref)

    for k in range(reads):
        feats[:, k * width : (k + 1) * width] = replies_ref[slots_ref[tile * reads + k]]
    for r in range(filters):
        part = dot(feats[...], radial_ref[0, :, r * probes : (r + 1) * probes])
        summed[r * channels : (r + 1) * channels, :] = (part * filter_weight(r, filters)).astype(BF16)
    hidden = dot(filter_ref[...], summed[...])
    gate = jax.nn.sigmoid(hidden)
    squashed = (hidden * gate).astype(BF16)
    mixed = dot(mix_ref[...], squashed)
    mixed_gate = jax.nn.sigmoid(mixed)
    outer = mixed * mixed_gate
    readout = jnp.broadcast_to(readout_ref[...], (8, channels)).T[:, :1]
    density = jnp.sum(readout * outer, axis=0, keepdims=True)
    density_ref[0] = density
    misfit = (density - target_ref[0]) / probes
    part = jnp.sum(outer * misfit, axis=1, keepdims=True)
    grad_readout_ref[...] += jnp.broadcast_to(part, (channels, channels)).T[:8, :]
    grad_mixed = (
        readout * misfit * (mixed_gate * (1.0 + mixed * (1.0 - mixed_gate)))
    ).astype(BF16)
    grad_mix_ref[...] += dot_nt(grad_mixed, squashed)
    grad_squashed = dot(mix_ref[...].T, grad_mixed)
    grad_hidden = (grad_squashed * (gate * (1.0 + hidden * (1.0 - gate)))).astype(BF16)
    grad_filter_ref[...] += dot_nt(grad_hidden, summed[...])
    grad_sums = dot(grad_hidden.T, filter_ref[...])
    for r in range(filters):
        part = grad_sums[:, r * channels : (r + 1) * channels] * filter_weight(r, filters)
        turned[r * probes : (r + 1) * probes, :] = part.astype(BF16)
    for k in range(reads):
        slot = slots_ref[tile * reads + k]
        back = dot(radial_ref[0, k * width : (k + 1) * width, :], turned[...])
        slot_total[slot] += back.T

    @pl.when(tile == tiles - 1)
    def _():
        slot_grad_ref[...] = slot_total[...].astype(BF16)


def final_kernel(ids_ref, returned_ref, where_ref, message_ref, sums_ref, grad_ref, totals):
    step = pl.program_id(0)
    group = sums_ref.shape[0]

    @pl.when(step == 0)
    def _():
        totals[...] = jnp.zeros_like(totals)

        def add(slot, carry):
            totals[ids_ref[slot]] += returned_ref[slot].astype(F32)
            return carry

        lax.fori_loop(0, returned_ref.shape[0], add, 0)

    grads = []
    for n in range(group):
        keep = where_ref[n].astype(F32)[3:4, :]
        grad = totals[step * group + n] * keep * silu_slope(message_ref[n])
        grads.append(grad.astype(BF16))
    part = dot_nt(
        jnp.concatenate(grads, axis=1),
        jnp.concatenate([sums_ref[n] for n in range(group)], axis=1),
    )

    @pl.when(step == 0)
    def _():
        grad_ref[...] = part

    @pl.when(step > 0)
    def _():
        grad_ref[...] += part


def reduce_kernel(axes, count, *refs):
    ins, outs = refs[:count], refs[count : 2 * count]
    total, sending, landing, gathered, send_sems, recv_sems = refs[2 * count :]
    rows, lanes = total.shape
    peers = []
    for axis, size in axes:
        here = lax.axis_index(axis)
        peers.append((here, [(here + d) % size for d in range(1, size)]))
    barrier = pltpu.get_barrier_semaphore()
    for (axis, _), (_, others) in zip(axes, peers):
        for other in others:
            pl.semaphore_signal(barrier, inc=1, device_id={axis: other}, device_id_type=MESH)
    pieces = []
    low = 0
    for index, ref in enumerate(ins):
        height = ref.shape[0]
        for left in range(0, ref.shape[1], lanes):
            total[low : low + height, :] = ref[:, left : left + lanes]
            pieces.append((index, left, low, height))
            low += height
    if low < rows:
        total[low:, :] = jnp.zeros((rows - low, lanes), F32)
    pl.semaphore_wait(barrier, sum(size - 1 for _, size in axes))
    sent = []

    def send(source, target, axis, other):
        n = len(sent)
        copy = pltpu.make_async_remote_copy(
            src_ref=source,
            dst_ref=target,
            send_sem=send_sems.at[n],
            recv_sem=recv_sems.at[n],
            device_id={axis: other},
            device_id_type=MESH,
        )
        copy.start()
        sent.append(copy)
        return copy

    start, extent, place, bases = 0, rows, 0, []
    for (axis, size), (here, others) in zip(axes, peers):
        sending[place : place + extent, :] = total[pl.ds(start, extent), :].astype(BF16)
        part = extent // size
        copies = []
        for d, other in enumerate(others):
            copies.append(
                send(
                    sending.at[pl.ds(pl.multiple_of(place + other * part, 16), part)],
                    landing.at[pl.ds(place + d * part, part)],
                    axis,
                    other,
                )
            )
        bases.append((start, extent))
        start = pl.multiple_of(start + here * part, 16)
        for d, copy in enumerate(copies):
            copy.wait_recv()
            total[pl.ds(start, part), :] += landing[
                place + d * part : place + (d + 1) * part, :
            ].astype(F32)
        place += extent
        extent = part
    gathered[pl.ds(start, extent), :] = total[pl.ds(start, extent), :].astype(BF16)
    for n in range(len(axes) - 1, -1, -1):
        axis = axes[n][0]
        mine = gathered.at[pl.ds(start, extent)]
        copies = [send(mine, mine, axis, other) for other in peers[n][1]]
        for copy in copies:
            copy.wait_recv()
        start, extent = bases[n]
    for index, left, low, height in pieces:
        padded = -(-height // 16) * 16
        part = gathered[low : low + padded, :].astype(F32)[:height]
        outs[index][:, left : left + lanes] = part
    for copy in sent:
        copy.wait_send()


def reduce_all(grads, axes, name, collective_id):
    devices = math.prod(size for _, size in axes)
    lanes = grads[0].shape[0]
    real = sum(-(-g.size // (16 * lanes)) * 16 for g in grads)
    rows = -(-real // (16 * devices)) * 16 * devices
    steps = sum(size - 1 for _, size in axes)
    spare = rows + rows // axes[0][1]
    vmem = pl.BlockSpec(memory_space=pltpu.VMEM)
    return pl.pallas_call(
        functools.partial(reduce_kernel, axes, len(grads)),
        in_specs=[vmem] * len(grads),
        out_specs=[vmem] * len(grads),
        out_shape=[jax.ShapeDtypeStruct(g.shape, F32) for g in grads],
        scratch_shapes=[
            pltpu.VMEM((rows, lanes), F32),
            pltpu.VMEM((spare, lanes), BF16),
            pltpu.VMEM((spare, lanes), BF16),
            pltpu.VMEM((rows, lanes), BF16),
            pltpu.SemaphoreType.DMA((2 * steps,)),
            pltpu.SemaphoreType.DMA((2 * steps,)),
        ],
        compiler_params=pltpu.CompilerParams(
            vmem_limit_bytes=VMEM_LIMIT, collective_id=collective_id, has_side_effects=True
        ),
        cost_estimate=cost(20e9),
        name=name,
    )(*grads)


def cost(flops):
    return pl.CostEstimate(flops=int(flops), bytes_accessed=1 << 20, transcendentals=0)


def whole(array):
    return pl.BlockSpec(array.shape, lambda *_: (0,) * array.ndim)


def body(
    atom_feat, atom_pos, atom_counts, atom_nbrs, probe_pos, probe_target, tile_blocks,
    atom_filter, probe_filter, mix_weight, readout,
):
    blocks, channels, width = atom_feat.shape
    tiles, reads = tile_blocks.shape
    probes = probe_pos.shape[2]
    filters = atom_filter.shape[1] // channels
    nbrs = atom_nbrs.shape[1]
    peers = lax.axis_size("tile")
    space_count = lax.axis_size("space")
    here = lax.axis_index("space")
    params = pltpu.CompilerParams(vmem_limit_bytes=VMEM_LIMIT)
    small = params
    mask = (jnp.arange(width)[None, :] < atom_counts[:, None]).astype(BF16)
    where = jnp.concatenate(
        [atom_pos, mask[:, None, :], jnp.zeros((blocks, 12, width), BF16)], axis=1
    )
    forward = [(i, (i + 1) % space_count) for i in range(space_count)]
    backward = [(b, a) for a, b in forward]
    low_feat = lax.ppermute(atom_feat, "space", forward)
    high_feat = lax.ppermute(atom_feat, "space", backward)
    around_where = jnp.concatenate(
        [lax.ppermute(where, "space", forward), where, lax.ppermute(where, "space", backward)],
        axis=0,
    )
    sides = ((atom_nbrs // (peers * blocks) - here + 1) % space_count).reshape(-1)
    near_rows = (atom_nbrs % blocks).reshape(-1)

    flat_owner = (tile_blocks // blocks % peers).reshape(-1)
    flat_spot = (tile_blocks % blocks).reshape(-1)
    cap = max(2, 2 * reads * tiles // peers)
    slots = peers * cap
    matches = (flat_owner[:, None, None] == jnp.arange(peers)[None, :, None]) & (
        flat_spot[:, None, None] == jnp.arange(blocks)[None, None, :]
    )
    needed = jnp.any(matches, axis=0).astype(jnp.int32)
    rank = jnp.cumsum(needed, axis=1) - needed
    chosen = (needed[:, None, :] == 1) & (rank[:, None, :] == jnp.arange(cap)[None, :, None])
    request_ids = jnp.sum(chosen.astype(jnp.int32) * jnp.arange(blocks)[None, None, :], axis=2)
    picked_rank = jnp.sum(jnp.where(matches, rank[None], 0), axis=(1, 2))
    slot_index = flat_owner * cap + picked_rank
    flat_where = jnp.broadcast_to(
        atom_pos.reshape(1, blocks * 3, width), (peers, blocks * 3, width)
    )
    asked_row = jnp.pad(request_ids.astype(BF16)[:, None, :], ((0, 0), (0, 15), (0, width - cap)))
    notes = lax.all_to_all(
        jnp.concatenate([flat_where, asked_row], axis=1), "tile",
        split_axis=0, concat_axis=0, tiled=True,
    )
    asked_ids = notes[:, blocks * 3, :cap].astype(jnp.int32).reshape(-1)
    group_where = notes[:, : blocks * 3, :].reshape(peers * blocks, 3, width)

    one = lambda b, *_: (b, 0, 0)
    atom_radial = pl.pallas_call(
        atom_radial_kernel,
        grid_spec=pltpu.PrefetchScalarGridSpec(
            num_scalar_prefetch=1,
            grid=(blocks,),
            in_specs=[whole(around_where), pl.BlockSpec((1, 16, width), one)],
            out_specs=pl.BlockSpec((1, nbrs * width, filters * width), one),
            scratch_shapes=[pltpu.VMEM((nbrs * width, 8), F32)],
        ),
        out_shape=jax.ShapeDtypeStruct((blocks, nbrs * width, filters * width), BF16),
        compiler_params=small,
        cost_estimate=cost(20e9),
        name="atom_radial",
    )(sides * blocks + near_rows, around_where, where)

    sent, sums, message = pl.pallas_call(
        atom_kernel,
        grid_spec=pltpu.PrefetchScalarGridSpec(
            num_scalar_prefetch=3,
            grid=(blocks,),
            in_specs=[
                whole(low_feat),
                whole(atom_feat),
                whole(high_feat),
                pl.BlockSpec((1, nbrs * width, filters * width), one),
                pl.BlockSpec((1, 16, width), one),
                whole(atom_filter),
            ],
            out_specs=[
                pl.BlockSpec((slots, channels, width), lambda *_: (0, 0, 0)),
                pl.BlockSpec((1, filters * channels, width), one),
                pl.BlockSpec((1, channels, width), one),
            ],
            scratch_shapes=[
                pltpu.VMEM((channels, nbrs * width), BF16),
                pltpu.VMEM((blocks, channels, width), BF16),
            ],
        ),
        out_shape=[
            jax.ShapeDtypeStruct((slots, channels, width), BF16),
            jax.ShapeDtypeStruct((blocks, filters * channels, width), BF16),
            jax.ShapeDtypeStruct((blocks, channels, width), F32),
        ],
        compiler_params=small,
        cost_estimate=cost(10e9),
        name="atom_layer",
    )(near_rows, sides, asked_ids, low_feat, atom_feat, high_feat, atom_radial, where, atom_filter)

    sent, group_where = lax.optimization_barrier((sent, group_where))
    replies = lax.all_to_all(
        sent.reshape(peers, cap, channels, width), "tile",
        split_axis=0, concat_axis=0, tiled=True,
    ).reshape(slots, channels, width)

    source_where = jnp.take(group_where, flat_owner * blocks + flat_spot, axis=0).astype(F32)
    source_where = jnp.pad(source_where, ((0, 0), (0, 5), (0, 0)))
    pieces = reads // 2
    per = reads // pieces
    probe_radial = pl.pallas_call(
        probe_radial_kernel,
        grid=(tiles, pieces),
        in_specs=[
            pl.BlockSpec((per, 8, width), lambda t, n: (t * pieces + n, 0, 0)),
            pl.BlockSpec((1, 3, probes), lambda t, n: (t, 0, 0)),
        ],
        out_specs=pl.BlockSpec((1, per * width, filters * probes), lambda t, n: (t, n, 0)),
        scratch_shapes=[pltpu.VMEM((per * width, 8), F32)],
        out_shape=jax.ShapeDtypeStruct((tiles, reads * width, filters * probes), BF16),
        compiler_params=small,
        cost_estimate=cost(20e9),
        name="probe_radial",
    )(source_where, probe_pos)

    readout_row = readout.reshape(1, channels)
    density, grad_filter, grad_mix, grad_readout, slot_grad = pl.pallas_call(
        probe_kernel,
        grid_spec=pltpu.PrefetchScalarGridSpec(
            num_scalar_prefetch=1,
            grid=(tiles,),
            in_specs=[
                whole(replies),
                pl.BlockSpec((1, reads * width, filters * probes), one),
                pl.BlockSpec((1, 1, probes), one),
                whole(probe_filter),
                whole(mix_weight),
                whole(readout_row),
            ],
            out_specs=[
                pl.BlockSpec((1, 1, probes), one),
                pl.BlockSpec((channels, filters * channels), lambda *_: (0, 0)),
                pl.BlockSpec((channels, channels), lambda *_: (0, 0)),
                pl.BlockSpec((8, channels), lambda *_: (0, 0)),
                pl.BlockSpec((slots, channels, width), lambda *_: (0, 0, 0)),
            ],
            scratch_shapes=[
                pltpu.VMEM((channels, reads * width), BF16),
                pltpu.VMEM((filters * channels, probes), BF16),
                pltpu.VMEM((filters * probes, channels), BF16),
                pltpu.VMEM((slots, channels, width), F32),
            ],
        ),
        out_shape=[
            jax.ShapeDtypeStruct((tiles, 1, probes), F32),
            jax.ShapeDtypeStruct((channels, filters * channels), F32),
            jax.ShapeDtypeStruct((channels, channels), F32),
            jax.ShapeDtypeStruct((8, channels), F32),
            jax.ShapeDtypeStruct((slots, channels, width), BF16),
        ],
        compiler_params=params,
        cost_estimate=cost(10e9),
        name="probe_layer",
    )(
        slot_index, replies, probe_radial, probe_target.reshape(tiles, 1, probes),
        probe_filter, mix_weight, readout_row,
    )

    returned = lax.all_to_all(
        slot_grad.reshape(peers, cap, channels, width), "tile",
        split_axis=0, concat_axis=0, tiled=True,
    ).reshape(slots, channels, width)
    axes = (("space", space_count), ("tile", peers))
    grad_filter, grad_mix, grad_readout = reduce_all(
        (grad_filter, grad_mix, grad_readout), axes, "probe_reduce", 0
    )
    group = math.gcd(blocks, 4)
    grad_atom = pl.pallas_call(
        final_kernel,
        grid_spec=pltpu.PrefetchScalarGridSpec(
            num_scalar_prefetch=1,
            grid=(blocks // group,),
            in_specs=[
                whole(returned),
                pl.BlockSpec((group, 16, width), one),
                pl.BlockSpec((group, channels, width), one),
                pl.BlockSpec((group, filters * channels, width), one),
            ],
            out_specs=pl.BlockSpec((channels, filters * channels), lambda *_: (0, 0)),
            scratch_shapes=[pltpu.VMEM((blocks, channels, width), F32)],
        ),
        out_shape=jax.ShapeDtypeStruct((channels, filters * channels), F32),
        compiler_params=params,
        cost_estimate=cost(10e9),
        name="atom_grad",
    )(asked_ids, returned, where, message, sums)
    (grad_atom,) = reduce_all((grad_atom,), axes, "atom_reduce", 1)
    return (density.reshape(tiles, probes), grad_atom, grad_filter, grad_mix, grad_readout[0])


def solution(mesh):
    return jax.shard_map(
        body,
        mesh=mesh,
        in_specs=(
            P(("space", "tile"), None, None),
            P(("space", "tile"), None, None),
            P(("space", "tile")),
            P(("space", "tile"), None),
            P(("space", "tile"), None, None),
            P(("space", "tile"), None),
            P(("space", "tile"), None),
            P(),
            P(),
            P(),
            P(),
        ),
        out_specs=(P(("space", "tile"), None), P(), P(), P(), P()),
        check_vma=False,
    )
```

```python
import functools
import math

import jax
import jax.numpy as jnp
from jax import lax
from jax.experimental import pallas as pl
from jax.experimental.pallas import tpu as pltpu
from jax.sharding import PartitionSpec as P

CUTOFF = 6.0
SPACING = 0.75
SPREAD = 0.75
LOG2E = 1.4426950408889634
MESH = pl.DeviceIdType.MESH
VMEM_LIMIT = 60 * 1024 * 1024
F32 = jnp.float32
BF16 = jnp.bfloat16


def silu_slope(values):
    s = jax.nn.sigmoid(values)
    return s * (1.0 + values * (1.0 - s))


def radial(source_cols, target_rows, factor, filters, keep=None):
    square = None
    for source, target in zip(source_cols, target_rows):
        offset = source - target
        square = offset * offset if square is None else square + offset * offset
    square = square + 0.01
    distance = square * lax.rsqrt(square)
    half = (math.pi / (2.0 * CUTOFF)) ** 2
    terms = [math.sqrt(factor) * (-half) ** k / math.factorial(2 * k) for k in range(7)]
    second = square * square
    wave = (terms[0] + terms[1] * square) + (terms[2] + terms[3] * square) * second
    wave = wave + ((terms[4] + terms[5] * square) + terms[6] * second) * (second * second)
    envelope = jnp.where(square < CUTOFF * CUTOFF, wave * wave, 0.0)
    middle = filters // 2
    shifted = distance * (1.0 / SPREAD) - middle * (SPACING / SPREAD)
    step = SPACING / SPREAD
    centre = envelope * jnp.exp2(shifted * shifted * (-LOG2E))
    if keep is not None:
        centre = centre * keep
    ratio = 2.0 * step * LOG2E
    up = jnp.exp2(shifted * ratio - step * step * LOG2E)
    down = jnp.exp2(shifted * (-ratio) - step * step * LOG2E)
    values = [None] * filters
    values[middle] = centre
    for r in range(middle + 1, filters):
        k = r - middle - 1
        values[r] = values[r - 1] * (up if k == 0 else up * math.exp(-2.0 * k * step * step))
    for r in range(middle - 1, -1, -1):
        k = middle - 1 - r
        values[r] = values[r + 1] * (down if k == 0 else down * math.exp(-2.0 * k * step * step))
    return values


def dot(a, b):
    return jnp.dot(a, b, preferred_element_type=F32)


def dot_nt(a, b):
    return lax.dot_general(a, b, (((1,), (1,)), ((), ())), preferred_element_type=F32)


def atom_radial_kernel(rows_ref, around_where_ref, own_where_ref, radial_ref, columns):
    block = pl.program_id(0)
    width = own_where_ref.shape[2]
    nbrs = radial_ref.shape[1] // width
    filters = radial_ref.shape[2] // width
    factor = (nbrs * width) ** (-0.5)
    own = own_where_ref[0].astype(F32)
    target = [own[c : c + 1, :] for c in range(3)]
    for k in range(nbrs):
        where = around_where_ref[rows_ref[block * nbrs + k]].astype(F32)
        columns[k * width : (k + 1) * width, :] = where[:8].T
    chunk = 32

    def fill(step, carry):
        start = pl.multiple_of(step * chunk, chunk)
        source = [columns[pl.ds(start, chunk), c : c + 1] for c in range(3)]
        keep = columns[pl.ds(start, chunk), 3:4]
        for r, value in enumerate(radial(source, target, factor, filters, keep)):
            radial_ref[0, pl.ds(start, chunk), r * width : (r + 1) * width] = value.astype(BF16)
        return carry

    lax.fori_loop(0, nbrs * width // chunk, fill, 0, unroll=4)


def atom_kernel(
    rows_ref, sides_ref, asked_ref, low_ref, own_ref, high_ref, radial_ref, where_ref, filter_ref,
    sent_ref, sums_ref, message_ref, feats, updated,
):
    block = pl.program_id(0)
    channels, width = own_ref.shape[1:]
    filters = filter_ref.shape[1] // channels
    nbrs = feats.shape[1] // width
    for k in range(nbrs):
        row = rows_ref[block * nbrs + k]
        part = (slice(None), slice(k * width, (k + 1) * width))
        if k < 3:
            feats[part] = (low_ref, high_ref, own_ref)[k][row]
            continue
        side = sides_ref[block * nbrs + k]
        for n, ref in enumerate((low_ref, own_ref, high_ref)):

            @pl.when(side == n)
            def _(ref=ref, row=row, part=part):
                feats[part] = ref[row]

    total = dot(feats[...], radial_ref[0])
    for r in range(filters):
        part = total[:, r * width : (r + 1) * width]
        sums_ref[0, r * channels : (r + 1) * channels, :] = part.astype(BF16)
    message = dot(filter_ref[...], sums_ref[0])
    message_ref[0] = message
    keep = where_ref[0].astype(F32)[3:4, :]
    fresh = (own_ref[block].astype(F32) + message * jax.nn.sigmoid(message)) * keep
    updated[block] = fresh.astype(BF16)

    @pl.when(block == pl.num_programs(0) - 1)
    def _():
        def pick(slot, carry):
            sent_ref[slot] = updated[asked_ref[slot]]
            return carry

        lax.fori_loop(0, sent_ref.shape[0], pick, 0)


def probe_radial_kernel(source_ref, where_ref, radial_ref, columns):
    width = source_ref.shape[2]
    reads = source_ref.shape[0]
    probes = where_ref.shape[2]
    filters = radial_ref.shape[2] // probes
    factor = (pl.num_programs(1) * reads * width) ** (-0.5)
    for k in range(reads):
        columns[k * width : (k + 1) * width, :] = source_ref[k].T
    chunk, span = 16, 256
    lanes = []
    for p in range(0, probes, span):
        lanes.append([where_ref[0, c : c + 1, p : p + span] for c in range(3)])

    def fill(step, carry):
        start = pl.multiple_of(step * chunk, chunk)
        source = [columns[pl.ds(start, chunk), c : c + 1] for c in range(3)]
        for n, target in enumerate(lanes):
            for r, value in enumerate(radial(source, target, factor, filters)):
                low = r * probes + n * span
                radial_ref[0, pl.ds(start, chunk), low : low + span] = value.astype(BF16)
        return carry

    lax.fori_loop(0, reads * width // chunk, fill, 0, unroll=2)


def probe_kernel(
    slots_ref, replies_ref, radial_ref, target_ref, filter_ref, mix_ref, readout_ref,
    density_ref, grad_filter_ref, grad_mix_ref, grad_readout_ref, slot_grad_ref,
    feats, summed, turned, slot_total,
):
    tile = pl.program_id(0)
    tiles = pl.num_programs(0)
    channels = mix_ref.shape[0]
    filters = filter_ref.shape[1] // channels
    width = replies_ref.shape[2]
    reads = feats.shape[1] // width
    probes = target_ref.shape[2]

    @pl.when(tile == 0)
    def _():
        slot_total[...] = jnp.zeros_like(slot_total)
        grad_filter_ref[...] = jnp.zeros_like(grad_filter_ref)
        grad_mix_ref[...] = jnp.zeros_like(grad_mix_ref)
        grad_readout_ref[...] = jnp.zeros_like(grad_readout_ref)

    for k in range(reads):
        feats[:, k * width : (k + 1) * width] = replies_ref[slots_ref[tile * reads + k]]
    for r in range(filters):
        part = dot(feats[...], radial_ref[0, :, r * probes : (r + 1) * probes])
        summed[r * channels : (r + 1) * channels, :] = (part).astype(BF16)
    hidden = dot(filter_ref[...], summed[...])
    gate = jax.nn.sigmoid(hidden)
    squashed = (hidden * gate).astype(BF16)
    mixed = dot(mix_ref[...], squashed)
    mixed_gate = jax.nn.sigmoid(mixed)
    outer = mixed * mixed_gate
    readout = jnp.broadcast_to(readout_ref[...], (8, channels)).T[:, :1]
    density = jnp.sum(readout * outer, axis=0, keepdims=True)
    density_ref[0] = density
    misfit = (density - target_ref[0]) / probes
    part = jnp.sum(outer * misfit, axis=1, keepdims=True)
    grad_readout_ref[...] += jnp.broadcast_to(part, (channels, channels)).T[:8, :]
    grad_mixed = (
        readout * misfit * (mixed_gate * (1.0 + mixed * (1.0 - mixed_gate)))
    ).astype(BF16)
    grad_mix_ref[...] += dot_nt(grad_mixed, squashed)
    grad_squashed = dot(mix_ref[...].T, grad_mixed)
    grad_hidden = (grad_squashed * (gate * (1.0 + hidden * (1.0 - gate)))).astype(BF16)
    grad_filter_ref[...] += dot_nt(grad_hidden, summed[...])
    grad_sums = dot(grad_hidden.T, filter_ref[...])
    for r in range(filters):
        part = grad_sums[:, r * channels : (r + 1) * channels]
        turned[r * probes : (r + 1) * probes, :] = part.astype(BF16)
    for k in range(reads):
        slot = slots_ref[tile * reads + k]
        back = dot(radial_ref[0, k * width : (k + 1) * width, :], turned[...])
        slot_total[slot] += back.T

    @pl.when(tile == tiles - 1)
    def _():
        slot_grad_ref[...] = slot_total[...].astype(BF16)


def final_kernel(ids_ref, returned_ref, where_ref, message_ref, sums_ref, grad_ref, totals):
    step = pl.program_id(0)
    group = sums_ref.shape[0]

    @pl.when(step == 0)
    def _():
        totals[...] = jnp.zeros_like(totals)

        def add(slot, carry):
            totals[ids_ref[slot]] += returned_ref[slot].astype(F32)
            return carry

        lax.fori_loop(0, returned_ref.shape[0], add, 0)

    grads = []
    for n in range(group):
        keep = where_ref[n].astype(F32)[3:4, :]
        grad = totals[step * group + n] * keep * silu_slope(message_ref[n])
        grads.append(grad.astype(BF16))
    part = dot_nt(
        jnp.concatenate(grads, axis=1),
        jnp.concatenate([sums_ref[n] for n in range(group)], axis=1),
    )

    @pl.when(step == 0)
    def _():
        grad_ref[...] = part

    @pl.when(step > 0)
    def _():
        grad_ref[...] += part


def reduce_kernel(axes, count, *refs):
    ins, outs = refs[:count], refs[count : 2 * count]
    total, sending, landing, gathered, send_sems, recv_sems = refs[2 * count :]
    rows, lanes = total.shape
    peers = []
    for axis, size in axes:
        here = lax.axis_index(axis)
        peers.append((here, [(here + d) % size for d in range(1, size)]))
    barrier = pltpu.get_barrier_semaphore()
    for (axis, _), (_, others) in zip(axes, peers):
        for other in others:
            pl.semaphore_signal(barrier, inc=1, device_id={axis: other}, device_id_type=MESH)
    pieces = []
    low = 0
    for index, ref in enumerate(ins):
        height = ref.shape[0]
        for left in range(0, ref.shape[1], lanes):
            total[low : low + height, :] = ref[:, left : left + lanes]
            pieces.append((index, left, low, height))
            low += height
    if low < rows:
        total[low:, :] = jnp.zeros((rows - low, lanes), F32)
    pl.semaphore_wait(barrier, sum(size - 1 for _, size in axes))
    sent = []

    def send(source, target, axis, other):
        n = len(sent)
        copy = pltpu.make_async_remote_copy(
            src_ref=source,
            dst_ref=target,
            send_sem=send_sems.at[n],
            recv_sem=recv_sems.at[n],
            device_id={axis: other},
            device_id_type=MESH,
        )
        copy.start()
        sent.append(copy)
        return copy

    start, extent, place, bases = 0, rows, 0, []
    for (axis, size), (here, others) in zip(axes, peers):
        sending[place : place + extent, :] = total[pl.ds(start, extent), :].astype(BF16)
        part = extent // size
        copies = []
        for d, other in enumerate(others):
            copies.append(
                send(
                    sending.at[pl.ds(pl.multiple_of(place + other * part, 16), part)],
                    landing.at[pl.ds(place + d * part, part)],
                    axis,
                    other,
                )
            )
        bases.append((start, extent))
        start = pl.multiple_of(start + here * part, 16)
        for d, copy in enumerate(copies):
            copy.wait_recv()
            total[pl.ds(start, part), :] += landing[
                place + d * part : place + (d + 1) * part, :
            ].astype(F32)
        place += extent
        extent = part
    gathered[pl.ds(start, extent), :] = total[pl.ds(start, extent), :].astype(BF16)
    for n in range(len(axes) - 1, -1, -1):
        axis = axes[n][0]
        mine = gathered.at[pl.ds(start, extent)]
        copies = [send(mine, mine, axis, other) for other in peers[n][1]]
        for copy in copies:
            copy.wait_recv()
        start, extent = bases[n]
    for index, left, low, height in pieces:
        padded = -(-height // 16) * 16
        part = gathered[low : low + padded, :].astype(F32)[:height]
        outs[index][:, left : left + lanes] = part
    for copy in sent:
        copy.wait_send()


def reduce_all(grads, axes, name, collective_id):
    devices = math.prod(size for _, size in axes)
    lanes = grads[0].shape[0]
    real = sum(-(-g.size // (16 * lanes)) * 16 for g in grads)
    rows = -(-real // (16 * devices)) * 16 * devices
    steps = sum(size - 1 for _, size in axes)
    spare = rows + rows // axes[0][1]
    vmem = pl.BlockSpec(memory_space=pltpu.VMEM)
    return pl.pallas_call(
        functools.partial(reduce_kernel, axes, len(grads)),
        in_specs=[vmem] * len(grads),
        out_specs=[vmem] * len(grads),
        out_shape=[jax.ShapeDtypeStruct(g.shape, F32) for g in grads],
        scratch_shapes=[
            pltpu.VMEM((rows, lanes), F32),
            pltpu.VMEM((spare, lanes), BF16),
            pltpu.VMEM((spare, lanes), BF16),
            pltpu.VMEM((rows, lanes), BF16),
            pltpu.SemaphoreType.DMA((2 * steps,)),
            pltpu.SemaphoreType.DMA((2 * steps,)),
        ],
        compiler_params=pltpu.CompilerParams(
            vmem_limit_bytes=VMEM_LIMIT, collective_id=collective_id, has_side_effects=True
        ),
        cost_estimate=cost(20e9),
        name=name,
    )(*grads)


def cost(flops):
    return pl.CostEstimate(flops=int(flops), bytes_accessed=1 << 20, transcendentals=0)


def whole(array):
    return pl.BlockSpec(array.shape, lambda *_: (0,) * array.ndim)


def body(
    atom_feat, atom_pos, atom_counts, atom_nbrs, probe_pos, probe_target, tile_blocks,
    atom_filter, probe_filter, mix_weight, readout,
):
    blocks, channels, width = atom_feat.shape
    tiles, reads = tile_blocks.shape
    probes = probe_pos.shape[2]
    filters = atom_filter.shape[1] // channels
    nbrs = atom_nbrs.shape[1]
    peers = lax.axis_size("tile")
    space_count = lax.axis_size("space")
    here = lax.axis_index("space")
    params = pltpu.CompilerParams(vmem_limit_bytes=VMEM_LIMIT)
    small = params
    mask = (jnp.arange(width)[None, :] < atom_counts[:, None]).astype(BF16)
    where = jnp.concatenate(
        [atom_pos, mask[:, None, :], jnp.zeros((blocks, 12, width), BF16)], axis=1
    )
    forward = [(i, (i + 1) % space_count) for i in range(space_count)]
    backward = [(b, a) for a, b in forward]
    low_feat = lax.ppermute(atom_feat, "space", forward)
    high_feat = lax.ppermute(atom_feat, "space", backward)
    around_where = jnp.concatenate(
        [lax.ppermute(where, "space", forward), where, lax.ppermute(where, "space", backward)],
        axis=0,
    )
    sides = ((atom_nbrs // (peers * blocks) - here + 1) % space_count).reshape(-1)
    near_rows = (atom_nbrs % blocks).reshape(-1)

    flat_owner = (tile_blocks // blocks % peers).reshape(-1)
    flat_spot = (tile_blocks % blocks).reshape(-1)
    cap = max(2, 2 * reads * tiles // peers)
    slots = peers * cap
    matches = (flat_owner[:, None, None] == jnp.arange(peers)[None, :, None]) & (
        flat_spot[:, None, None] == jnp.arange(blocks)[None, None, :]
    )
    needed = jnp.any(matches, axis=0).astype(jnp.int32)
    rank = jnp.cumsum(needed, axis=1) - needed
    chosen = (needed[:, None, :] == 1) & (rank[:, None, :] == jnp.arange(cap)[None, :, None])
    request_ids = jnp.sum(chosen.astype(jnp.int32) * jnp.arange(blocks)[None, None, :], axis=2)
    picked_rank = jnp.sum(jnp.where(matches, rank[None], 0), axis=(1, 2))
    slot_index = flat_owner * cap + picked_rank
    flat_where = jnp.broadcast_to(
        atom_pos.reshape(1, blocks * 3, width), (peers, blocks * 3, width)
    )
    asked_row = jnp.pad(request_ids.astype(BF16)[:, None, :], ((0, 0), (0, 15), (0, width - cap)))
    notes = lax.all_to_all(
        jnp.concatenate([flat_where, asked_row], axis=1), "tile",
        split_axis=0, concat_axis=0, tiled=True,
    )
    asked_ids = notes[:, blocks * 3, :cap].astype(jnp.int32).reshape(-1)
    group_where = notes[:, : blocks * 3, :].reshape(peers * blocks, 3, width)

    one = lambda b, *_: (b, 0, 0)
    atom_radial = pl.pallas_call(
        atom_radial_kernel,
        grid_spec=pltpu.PrefetchScalarGridSpec(
            num_scalar_prefetch=1,
            grid=(blocks,),
            in_specs=[whole(around_where), pl.BlockSpec((1, 16, width), one)],
            out_specs=pl.BlockSpec((1, nbrs * width, filters * width), one),
            scratch_shapes=[pltpu.VMEM((nbrs * width, 8), F32)],
        ),
        out_shape=jax.ShapeDtypeStruct((blocks, nbrs * width, filters * width), BF16),
        compiler_params=small,
        cost_estimate=cost(20e9),
        name="atom_radial",
    )(sides * blocks + near_rows, around_where, where)

    sent, sums, message = pl.pallas_call(
        atom_kernel,
        grid_spec=pltpu.PrefetchScalarGridSpec(
            num_scalar_prefetch=3,
            grid=(blocks,),
            in_specs=[
                whole(low_feat),
                whole(atom_feat),
                whole(high_feat),
                pl.BlockSpec((1, nbrs * width, filters * width), one),
                pl.BlockSpec((1, 16, width), one),
                whole(atom_filter),
            ],
            out_specs=[
                pl.BlockSpec((slots, channels, width), lambda *_: (0, 0, 0)),
                pl.BlockSpec((1, filters * channels, width), one),
                pl.BlockSpec((1, channels, width), one),
            ],
            scratch_shapes=[
                pltpu.VMEM((channels, nbrs * width), BF16),
                pltpu.VMEM((blocks, channels, width), BF16),
            ],
        ),
        out_shape=[
            jax.ShapeDtypeStruct((slots, channels, width), BF16),
            jax.ShapeDtypeStruct((blocks, filters * channels, width), BF16),
            jax.ShapeDtypeStruct((blocks, channels, width), F32),
        ],
        compiler_params=small,
        cost_estimate=cost(10e9),
        name="atom_layer",
    )(near_rows, sides, asked_ids, low_feat, atom_feat, high_feat, atom_radial, where, atom_filter)

    sent, group_where = lax.optimization_barrier((sent, group_where))
    replies = lax.all_to_all(
        sent.reshape(peers, cap, channels, width), "tile",
        split_axis=0, concat_axis=0, tiled=True,
    ).reshape(slots, channels, width)

    source_where = jnp.take(group_where, flat_owner * blocks + flat_spot, axis=0).astype(F32)
    source_where = jnp.pad(source_where, ((0, 0), (0, 5), (0, 0)))
    pieces = reads // 2
    per = reads // pieces
    probe_radial = pl.pallas_call(
        probe_radial_kernel,
        grid=(tiles, pieces),
        in_specs=[
            pl.BlockSpec((per, 8, width), lambda t, n: (t * pieces + n, 0, 0)),
            pl.BlockSpec((1, 3, probes), lambda t, n: (t, 0, 0)),
        ],
        out_specs=pl.BlockSpec((1, per * width, filters * probes), lambda t, n: (t, n, 0)),
        scratch_shapes=[pltpu.VMEM((per * width, 8), F32)],
        out_shape=jax.ShapeDtypeStruct((tiles, reads * width, filters * probes), BF16),
        compiler_params=small,
        cost_estimate=cost(20e9),
        name="probe_radial",
    )(source_where, probe_pos)

    readout_row = readout.reshape(1, channels)
    density, grad_filter, grad_mix, grad_readout, slot_grad = pl.pallas_call(
        probe_kernel,
        grid_spec=pltpu.PrefetchScalarGridSpec(
            num_scalar_prefetch=1,
            grid=(tiles,),
            in_specs=[
                whole(replies),
                pl.BlockSpec((1, reads * width, filters * probes), one),
                pl.BlockSpec((1, 1, probes), one),
                whole(probe_filter),
                whole(mix_weight),
                whole(readout_row),
            ],
            out_specs=[
                pl.BlockSpec((1, 1, probes), one),
                pl.BlockSpec((channels, filters * channels), lambda *_: (0, 0)),
                pl.BlockSpec((channels, channels), lambda *_: (0, 0)),
                pl.BlockSpec((8, channels), lambda *_: (0, 0)),
                pl.BlockSpec((slots, channels, width), lambda *_: (0, 0, 0)),
            ],
            scratch_shapes=[
                pltpu.VMEM((channels, reads * width), BF16),
                pltpu.VMEM((filters * channels, probes), BF16),
                pltpu.VMEM((filters * probes, channels), BF16),
                pltpu.VMEM((slots, channels, width), F32),
            ],
        ),
        out_shape=[
            jax.ShapeDtypeStruct((tiles, 1, probes), F32),
            jax.ShapeDtypeStruct((channels, filters * channels), F32),
            jax.ShapeDtypeStruct((channels, channels), F32),
            jax.ShapeDtypeStruct((8, channels), F32),
            jax.ShapeDtypeStruct((slots, channels, width), BF16),
        ],
        compiler_params=params,
        cost_estimate=cost(10e9),
        name="probe_layer",
    )(
        slot_index, replies, probe_radial, probe_target.reshape(tiles, 1, probes),
        probe_filter, mix_weight, readout_row,
    )

    returned = lax.all_to_all(
        slot_grad.reshape(peers, cap, channels, width), "tile",
        split_axis=0, concat_axis=0, tiled=True,
    ).reshape(slots, channels, width)
    axes = (("space", space_count), ("tile", peers))
    group = math.gcd(blocks, 4)
    grad_atom = pl.pallas_call(
        final_kernel,
        grid_spec=pltpu.PrefetchScalarGridSpec(
            num_scalar_prefetch=1,
            grid=(blocks // group,),
            in_specs=[
                whole(returned),
                pl.BlockSpec((group, 16, width), one),
                pl.BlockSpec((group, channels, width), one),
                pl.BlockSpec((group, filters * channels, width), one),
            ],
            out_specs=pl.BlockSpec((channels, filters * channels), lambda *_: (0, 0)),
            scratch_shapes=[pltpu.VMEM((blocks, channels, width), F32)],
        ),
        out_shape=jax.ShapeDtypeStruct((channels, filters * channels), F32),
        compiler_params=params,
        cost_estimate=cost(10e9),
        name="atom_grad",
    )(asked_ids, returned, where, message, sums)
    grad_atom, grad_filter, grad_mix, grad_readout = reduce_all(
        (grad_atom, grad_filter, grad_mix, grad_readout), axes, "grad_reduce", 0
    )
    return (density.reshape(tiles, probes), grad_atom, grad_filter, grad_mix, grad_readout[0])


def solution(mesh):
    return jax.shard_map(
        body,
        mesh=mesh,
        in_specs=(
            P(("space", "tile"), None, None),
            P(("space", "tile"), None, None),
            P(("space", "tile")),
            P(("space", "tile"), None),
            P(("space", "tile"), None, None),
            P(("space", "tile"), None),
            P(("space", "tile"), None),
            P(),
            P(),
            P(),
            P(),
        ),
        out_specs=(P(("space", "tile"), None), P(), P(), P(), P()),
        check_vma=False,
    )
```

```python
import functools
import math

import jax
import jax.numpy as jnp
from jax import lax
from jax.experimental import pallas as pl
from jax.experimental.pallas import tpu as pltpu
from jax.sharding import PartitionSpec as P

CUTOFF = 6.0
SPACING = 0.75
SPREAD = 0.75
LOG2E = 1.4426950408889634
MESH = pl.DeviceIdType.MESH
VMEM_LIMIT = 60 * 1024 * 1024
F32 = jnp.float32
BF16 = jnp.bfloat16


def silu_slope(values):
    s = jax.nn.sigmoid(values)
    return s * (1.0 + values * (1.0 - s))


def radial(source_cols, target_rows, factor, filters, keep=None):
    square = None
    for source, target in zip(source_cols, target_rows):
        offset = source - target
        square = offset * offset if square is None else square + offset * offset
    square = square + 0.01
    distance = square * lax.rsqrt(square)
    half = (math.pi / (2.0 * CUTOFF)) ** 2
    terms = [math.sqrt(factor) * (-half) ** k / math.factorial(2 * k) for k in range(7)]
    second = square * square
    wave = (terms[0] + terms[1] * square) + (terms[2] + terms[3] * square) * second
    wave = wave + ((terms[4] + terms[5] * square) + terms[6] * second) * (second * second)
    envelope = jnp.where(square < CUTOFF * CUTOFF, wave * wave, 0.0)
    middle = filters // 2
    shifted = distance * (1.0 / SPREAD) - middle * (SPACING / SPREAD)
    step = SPACING / SPREAD
    centre = envelope * jnp.exp2(shifted * shifted * (-LOG2E))
    if keep is not None:
        centre = centre * keep
    ratio = 2.0 * step * LOG2E
    up = jnp.exp2(shifted * ratio - step * step * LOG2E)
    down = jnp.exp2(shifted * (-ratio) - step * step * LOG2E)
    values = [None] * filters
    values[middle] = centre
    for r in range(middle + 1, filters):
        k = r - middle - 1
        values[r] = values[r - 1] * (up if k == 0 else up * math.exp(-2.0 * k * step * step))
    for r in range(middle - 1, -1, -1):
        k = middle - 1 - r
        values[r] = values[r + 1] * (down if k == 0 else down * math.exp(-2.0 * k * step * step))
    return values


def dot(a, b):
    return jnp.dot(a, b, preferred_element_type=F32)


def dot_nt(a, b):
    return lax.dot_general(a, b, (((1,), (1,)), ((), ())), preferred_element_type=F32)


def atom_radial_kernel(rows_ref, around_where_ref, own_where_ref, radial_ref, columns):
    block = pl.program_id(0)
    width = own_where_ref.shape[2]
    nbrs = radial_ref.shape[1] // width
    filters = radial_ref.shape[2] // width
    factor = (nbrs * width) ** (-0.5)
    own = own_where_ref[0].astype(F32)
    target = [own[c : c + 1, :] for c in range(3)]
    for k in range(nbrs):
        where = around_where_ref[rows_ref[block * nbrs + k]].astype(F32)
        columns[k * width : (k + 1) * width, :] = where[:8].T
    chunk = 32

    def fill(step, carry):
        start = pl.multiple_of(step * chunk, chunk)
        source = [columns[pl.ds(start, chunk), c : c + 1] for c in range(3)]
        keep = columns[pl.ds(start, chunk), 3:4]
        for r, value in enumerate(radial(source, target, factor, filters, keep)):
            radial_ref[0, pl.ds(start, chunk), r * width : (r + 1) * width] = value.astype(BF16)
        return carry

    lax.fori_loop(0, nbrs * width // chunk, fill, 0, unroll=8)


def atom_kernel(
    rows_ref, sides_ref, asked_ref, low_ref, own_ref, high_ref, radial_ref, where_ref, filter_ref,
    sent_ref, sums_ref, message_ref, feats, updated,
):
    block = pl.program_id(0)
    channels, width = own_ref.shape[1:]
    filters = filter_ref.shape[1] // channels
    nbrs = feats.shape[1] // width
    for k in range(nbrs):
        row = rows_ref[block * nbrs + k]
        part = (slice(None), slice(k * width, (k + 1) * width))
        if k < 3:
            feats[part] = (low_ref, high_ref, own_ref)[k][row]
            continue
        side = sides_ref[block * nbrs + k]
        for n, ref in enumerate((low_ref, own_ref, high_ref)):

            @pl.when(side == n)
            def _(ref=ref, row=row, part=part):
                feats[part] = ref[row]

    total = dot(feats[...], radial_ref[0])
    for r in range(filters):
        part = total[:, r * width : (r + 1) * width]
        sums_ref[0, r * channels : (r + 1) * channels, :] = part.astype(BF16)
    message = dot(filter_ref[...], sums_ref[0])
    message_ref[0] = message
    keep = where_ref[0].astype(F32)[3:4, :]
    fresh = (own_ref[block].astype(F32) + message * jax.nn.sigmoid(message)) * keep
    updated[block] = fresh.astype(BF16)

    @pl.when(block == pl.num_programs(0) - 1)
    def _():
        def pick(slot, carry):
            sent_ref[slot] = updated[asked_ref[slot]]
            return carry

        lax.fori_loop(0, sent_ref.shape[0], pick, 0)


def probe_radial_kernel(source_ref, where_ref, radial_ref, columns):
    width = source_ref.shape[2]
    reads = source_ref.shape[0]
    probes = where_ref.shape[2]
    filters = radial_ref.shape[2] // probes
    factor = (pl.num_programs(1) * reads * width) ** (-0.5)
    for k in range(reads):
        columns[k * width : (k + 1) * width, :] = source_ref[k].T
    chunk, span = 16, 256
    lanes = []
    for p in range(0, probes, span):
        lanes.append([where_ref[0, c : c + 1, p : p + span] for c in range(3)])

    def fill(step, carry):
        start = pl.multiple_of(step * chunk, chunk)
        source = [columns[pl.ds(start, chunk), c : c + 1] for c in range(3)]
        for n, target in enumerate(lanes):
            for r, value in enumerate(radial(source, target, factor, filters)):
                low = r * probes + n * span
                radial_ref[0, pl.ds(start, chunk), low : low + span] = value.astype(BF16)
        return carry

    lax.fori_loop(0, reads * width // chunk, fill, 0, unroll=4)


def probe_kernel(
    slots_ref, replies_ref, radial_ref, target_ref, filter_ref, mix_ref, readout_ref,
    density_ref, grad_filter_ref, grad_mix_ref, grad_readout_ref, slot_grad_ref,
    feats, summed, turned, slot_total,
):
    tile = pl.program_id(0)
    tiles = pl.num_programs(0)
    channels = mix_ref.shape[0]
    filters = filter_ref.shape[1] // channels
    width = replies_ref.shape[2]
    reads = feats.shape[1] // width
    probes = target_ref.shape[2]

    @pl.when(tile == 0)
    def _():
        slot_total[...] = jnp.zeros_like(slot_total)
        grad_filter_ref[...] = jnp.zeros_like(grad_filter_ref)
        grad_mix_ref[...] = jnp.zeros_like(grad_mix_ref)
        grad_readout_ref[...] = jnp.zeros_like(grad_readout_ref)

    for k in range(reads):
        feats[:, k * width : (k + 1) * width] = replies_ref[slots_ref[tile * reads + k]]
    for r in range(filters):
        part = dot(feats[...], radial_ref[0, :, r * probes : (r + 1) * probes])
        summed[r * channels : (r + 1) * channels, :] = (part).astype(BF16)
    hidden = dot(filter_ref[...], summed[...])
    gate = jax.nn.sigmoid(hidden)
    squashed = (hidden * gate).astype(BF16)
    mixed = dot(mix_ref[...], squashed)
    mixed_gate = jax.nn.sigmoid(mixed)
    outer = mixed * mixed_gate
    readout = jnp.broadcast_to(readout_ref[...], (8, channels)).T[:, :1]
    density = jnp.sum(readout * outer, axis=0, keepdims=True)
    density_ref[0] = density
    misfit = (density - target_ref[0]) / probes
    part = jnp.sum(outer * misfit, axis=1, keepdims=True)
    grad_readout_ref[...] += jnp.broadcast_to(part, (channels, channels)).T[:8, :]
    grad_mixed = (
        readout * misfit * (mixed_gate * (1.0 + mixed * (1.0 - mixed_gate)))
    ).astype(BF16)
    grad_mix_ref[...] += dot_nt(grad_mixed, squashed)
    grad_squashed = dot(mix_ref[...].T, grad_mixed)
    grad_hidden = (grad_squashed * (gate * (1.0 + hidden * (1.0 - gate)))).astype(BF16)
    grad_filter_ref[...] += dot_nt(grad_hidden, summed[...])
    grad_sums = dot(grad_hidden.T, filter_ref[...])
    for r in range(filters):
        part = grad_sums[:, r * channels : (r + 1) * channels]
        turned[r * probes : (r + 1) * probes, :] = part.astype(BF16)
    for k in range(reads):
        slot = slots_ref[tile * reads + k]
        back = dot(radial_ref[0, k * width : (k + 1) * width, :], turned[...])
        slot_total[slot] += back.T

    @pl.when(tile == tiles - 1)
    def _():
        slot_grad_ref[...] = slot_total[...].astype(BF16)


def final_kernel(ids_ref, returned_ref, where_ref, message_ref, sums_ref, grad_ref, totals):
    step = pl.program_id(0)
    group = sums_ref.shape[0]

    @pl.when(step == 0)
    def _():
        totals[...] = jnp.zeros_like(totals)

        def add(slot, carry):
            totals[ids_ref[slot]] += returned_ref[slot].astype(F32)
            return carry

        lax.fori_loop(0, returned_ref.shape[0], add, 0)

    grads = []
    for n in range(group):
        keep = where_ref[n].astype(F32)[3:4, :]
        grad = totals[step * group + n] * keep * silu_slope(message_ref[n])
        grads.append(grad.astype(BF16))
    part = dot_nt(
        jnp.concatenate(grads, axis=1),
        jnp.concatenate([sums_ref[n] for n in range(group)], axis=1),
    )

    @pl.when(step == 0)
    def _():
        grad_ref[...] = part

    @pl.when(step > 0)
    def _():
        grad_ref[...] += part


def reduce_kernel(axes, count, *refs):
    ins, outs = refs[:count], refs[count : 2 * count]
    total, sending, landing, gathered, send_sems, recv_sems = refs[2 * count :]
    rows, lanes = total.shape
    peers = []
    for axis, size in axes:
        here = lax.axis_index(axis)
        peers.append((here, [(here + d) % size for d in range(1, size)]))
    barrier = pltpu.get_barrier_semaphore()
    for (axis, _), (_, others) in zip(axes, peers):
        for other in others:
            pl.semaphore_signal(barrier, inc=1, device_id={axis: other}, device_id_type=MESH)
    pieces = []
    low = 0
    for index, ref in enumerate(ins):
        height = ref.shape[0]
        for left in range(0, ref.shape[1], lanes):
            total[low : low + height, :] = ref[:, left : left + lanes]
            pieces.append((index, left, low, height))
            low += height
    if low < rows:
        total[low:, :] = jnp.zeros((rows - low, lanes), F32)
    pl.semaphore_wait(barrier, sum(size - 1 for _, size in axes))
    sent = []

    def send(source, target, axis, other):
        n = len(sent)
        copy = pltpu.make_async_remote_copy(
            src_ref=source,
            dst_ref=target,
            send_sem=send_sems.at[n],
            recv_sem=recv_sems.at[n],
            device_id={axis: other},
            device_id_type=MESH,
        )
        copy.start()
        sent.append(copy)
        return copy

    start, extent, place, bases = 0, rows, 0, []
    for (axis, size), (here, others) in zip(axes, peers):
        sending[place : place + extent, :] = total[pl.ds(start, extent), :].astype(BF16)
        part = extent // size
        copies = []
        for d, other in enumerate(others):
            copies.append(
                send(
                    sending.at[pl.ds(pl.multiple_of(place + other * part, 16), part)],
                    landing.at[pl.ds(place + d * part, part)],
                    axis,
                    other,
                )
            )
        bases.append((start, extent))
        start = pl.multiple_of(start + here * part, 16)
        for d, copy in enumerate(copies):
            copy.wait_recv()
            total[pl.ds(start, part), :] += landing[
                place + d * part : place + (d + 1) * part, :
            ].astype(F32)
        place += extent
        extent = part
    gathered[pl.ds(start, extent), :] = total[pl.ds(start, extent), :].astype(BF16)
    for n in range(len(axes) - 1, -1, -1):
        axis = axes[n][0]
        mine = gathered.at[pl.ds(start, extent)]
        copies = [send(mine, mine, axis, other) for other in peers[n][1]]
        for copy in copies:
            copy.wait_recv()
        start, extent = bases[n]
    for index, left, low, height in pieces:
        padded = -(-height // 16) * 16
        part = gathered[low : low + padded, :].astype(F32)[:height]
        outs[index][:, left : left + lanes] = part
    for copy in sent:
        copy.wait_send()


def reduce_all(grads, axes, name, collective_id):
    devices = math.prod(size for _, size in axes)
    lanes = grads[0].shape[0]
    real = sum(-(-g.size // (16 * lanes)) * 16 for g in grads)
    rows = -(-real // (16 * devices)) * 16 * devices
    steps = sum(size - 1 for _, size in axes)
    spare = rows + rows // axes[0][1]
    vmem = pl.BlockSpec(memory_space=pltpu.VMEM)
    return pl.pallas_call(
        functools.partial(reduce_kernel, axes, len(grads)),
        in_specs=[vmem] * len(grads),
        out_specs=[vmem] * len(grads),
        out_shape=[jax.ShapeDtypeStruct(g.shape, F32) for g in grads],
        scratch_shapes=[
            pltpu.VMEM((rows, lanes), F32),
            pltpu.VMEM((spare, lanes), BF16),
            pltpu.VMEM((spare, lanes), BF16),
            pltpu.VMEM((rows, lanes), BF16),
            pltpu.SemaphoreType.DMA((2 * steps,)),
            pltpu.SemaphoreType.DMA((2 * steps,)),
        ],
        compiler_params=pltpu.CompilerParams(
            vmem_limit_bytes=VMEM_LIMIT, collective_id=collective_id, has_side_effects=True
        ),
        cost_estimate=cost(20e9),
        name=name,
    )(*grads)


def cost(flops):
    return pl.CostEstimate(flops=int(flops), bytes_accessed=1 << 20, transcendentals=0)


def whole(array):
    return pl.BlockSpec(array.shape, lambda *_: (0,) * array.ndim)


def body(
    atom_feat, atom_pos, atom_counts, atom_nbrs, probe_pos, probe_target, tile_blocks,
    atom_filter, probe_filter, mix_weight, readout,
):
    blocks, channels, width = atom_feat.shape
    tiles, reads = tile_blocks.shape
    probes = probe_pos.shape[2]
    filters = atom_filter.shape[1] // channels
    nbrs = atom_nbrs.shape[1]
    peers = lax.axis_size("tile")
    space_count = lax.axis_size("space")
    here = lax.axis_index("space")
    params = pltpu.CompilerParams(vmem_limit_bytes=VMEM_LIMIT)
    small = params
    mask = (jnp.arange(width)[None, :] < atom_counts[:, None]).astype(BF16)
    where = jnp.concatenate(
        [atom_pos, mask[:, None, :], jnp.zeros((blocks, 12, width), BF16)], axis=1
    )
    forward = [(i, (i + 1) % space_count) for i in range(space_count)]
    backward = [(b, a) for a, b in forward]
    low_feat = lax.ppermute(atom_feat, "space", forward)
    high_feat = lax.ppermute(atom_feat, "space", backward)
    around_where = jnp.concatenate(
        [lax.ppermute(where, "space", forward), where, lax.ppermute(where, "space", backward)],
        axis=0,
    )
    sides = ((atom_nbrs // (peers * blocks) - here + 1) % space_count).reshape(-1)
    near_rows = (atom_nbrs % blocks).reshape(-1)

    flat_owner = (tile_blocks // blocks % peers).reshape(-1)
    flat_spot = (tile_blocks % blocks).reshape(-1)
    cap = max(2, 2 * reads * tiles // peers)
    slots = peers * cap
    matches = (flat_owner[:, None, None] == jnp.arange(peers)[None, :, None]) & (
        flat_spot[:, None, None] == jnp.arange(blocks)[None, None, :]
    )
    needed = jnp.any(matches, axis=0).astype(jnp.int32)
    rank = jnp.cumsum(needed, axis=1) - needed
    chosen = (needed[:, None, :] == 1) & (rank[:, None, :] == jnp.arange(cap)[None, :, None])
    request_ids = jnp.sum(chosen.astype(jnp.int32) * jnp.arange(blocks)[None, None, :], axis=2)
    picked_rank = jnp.sum(jnp.where(matches, rank[None], 0), axis=(1, 2))
    slot_index = flat_owner * cap + picked_rank
    flat_where = jnp.broadcast_to(
        atom_pos.reshape(1, blocks * 3, width), (peers, blocks * 3, width)
    )
    asked_row = jnp.pad(request_ids.astype(BF16)[:, None, :], ((0, 0), (0, 15), (0, width - cap)))
    notes = lax.all_to_all(
        jnp.concatenate([flat_where, asked_row], axis=1), "tile",
        split_axis=0, concat_axis=0, tiled=True,
    )
    asked_ids = notes[:, blocks * 3, :cap].astype(jnp.int32).reshape(-1)
    group_where = notes[:, : blocks * 3, :].reshape(peers * blocks, 3, width)

    one = lambda b, *_: (b, 0, 0)
    atom_radial = pl.pallas_call(
        atom_radial_kernel,
        grid_spec=pltpu.PrefetchScalarGridSpec(
            num_scalar_prefetch=1,
            grid=(blocks,),
            in_specs=[whole(around_where), pl.BlockSpec((1, 16, width), one)],
            out_specs=pl.BlockSpec((1, nbrs * width, filters * width), one),
            scratch_shapes=[pltpu.VMEM((nbrs * width, 8), F32)],
        ),
        out_shape=jax.ShapeDtypeStruct((blocks, nbrs * width, filters * width), BF16),
        compiler_params=small,
        cost_estimate=cost(20e9),
        name="atom_radial",
    )(sides * blocks + near_rows, around_where, where)

    sent, sums, message = pl.pallas_call(
        atom_kernel,
        grid_spec=pltpu.PrefetchScalarGridSpec(
            num_scalar_prefetch=3,
            grid=(blocks,),
            in_specs=[
                whole(low_feat),
                whole(atom_feat),
                whole(high_feat),
                pl.BlockSpec((1, nbrs * width, filters * width), one),
                pl.BlockSpec((1, 16, width), one),
                whole(atom_filter),
            ],
            out_specs=[
                pl.BlockSpec((slots, channels, width), lambda *_: (0, 0, 0)),
                pl.BlockSpec((1, filters * channels, width), one),
                pl.BlockSpec((1, channels, width), one),
            ],
            scratch_shapes=[
                pltpu.VMEM((channels, nbrs * width), BF16),
                pltpu.VMEM((blocks, channels, width), BF16),
            ],
        ),
        out_shape=[
            jax.ShapeDtypeStruct((slots, channels, width), BF16),
            jax.ShapeDtypeStruct((blocks, filters * channels, width), BF16),
            jax.ShapeDtypeStruct((blocks, channels, width), F32),
        ],
        compiler_params=small,
        cost_estimate=cost(10e9),
        name="atom_layer",
    )(near_rows, sides, asked_ids, low_feat, atom_feat, high_feat, atom_radial, where, atom_filter)

    sent, group_where = lax.optimization_barrier((sent, group_where))
    replies = lax.all_to_all(
        sent.reshape(peers, cap, channels, width), "tile",
        split_axis=0, concat_axis=0, tiled=True,
    ).reshape(slots, channels, width)

    source_where = jnp.take(group_where, flat_owner * blocks + flat_spot, axis=0).astype(F32)
    source_where = jnp.pad(source_where, ((0, 0), (0, 5), (0, 0)))
    pieces = reads // 2
    per = reads // pieces
    probe_radial = pl.pallas_call(
        probe_radial_kernel,
        grid=(tiles, pieces),
        in_specs=[
            pl.BlockSpec((per, 8, width), lambda t, n: (t * pieces + n, 0, 0)),
            pl.BlockSpec((1, 3, probes), lambda t, n: (t, 0, 0)),
        ],
        out_specs=pl.BlockSpec((1, per * width, filters * probes), lambda t, n: (t, n, 0)),
        scratch_shapes=[pltpu.VMEM((per * width, 8), F32)],
        out_shape=jax.ShapeDtypeStruct((tiles, reads * width, filters * probes), BF16),
        compiler_params=small,
        cost_estimate=cost(20e9),
        name="probe_radial",
    )(source_where, probe_pos)

    readout_row = readout.reshape(1, channels)
    density, grad_filter, grad_mix, grad_readout, slot_grad = pl.pallas_call(
        probe_kernel,
        grid_spec=pltpu.PrefetchScalarGridSpec(
            num_scalar_prefetch=1,
            grid=(tiles,),
            in_specs=[
                whole(replies),
                pl.BlockSpec((1, reads * width, filters * probes), one),
                pl.BlockSpec((1, 1, probes), one),
                whole(probe_filter),
                whole(mix_weight),
                whole(readout_row),
            ],
            out_specs=[
                pl.BlockSpec((1, 1, probes), one),
                pl.BlockSpec((channels, filters * channels), lambda *_: (0, 0)),
                pl.BlockSpec((channels, channels), lambda *_: (0, 0)),
                pl.BlockSpec((8, channels), lambda *_: (0, 0)),
                pl.BlockSpec((slots, channels, width), lambda *_: (0, 0, 0)),
            ],
            scratch_shapes=[
                pltpu.VMEM((channels, reads * width), BF16),
                pltpu.VMEM((filters * channels, probes), BF16),
                pltpu.VMEM((filters * probes, channels), BF16),
                pltpu.VMEM((slots, channels, width), F32),
            ],
        ),
        out_shape=[
            jax.ShapeDtypeStruct((tiles, 1, probes), F32),
            jax.ShapeDtypeStruct((channels, filters * channels), F32),
            jax.ShapeDtypeStruct((channels, channels), F32),
            jax.ShapeDtypeStruct((8, channels), F32),
            jax.ShapeDtypeStruct((slots, channels, width), BF16),
        ],
        compiler_params=params,
        cost_estimate=cost(10e9),
        name="probe_layer",
    )(
        slot_index, replies, probe_radial, probe_target.reshape(tiles, 1, probes),
        probe_filter, mix_weight, readout_row,
    )

    returned = lax.all_to_all(
        slot_grad.reshape(peers, cap, channels, width), "tile",
        split_axis=0, concat_axis=0, tiled=True,
    ).reshape(slots, channels, width)
    axes = (("space", space_count), ("tile", peers))
    group = math.gcd(blocks, 4)
    grad_atom = pl.pallas_call(
        final_kernel,
        grid_spec=pltpu.PrefetchScalarGridSpec(
            num_scalar_prefetch=1,
            grid=(blocks // group,),
            in_specs=[
                whole(returned),
                pl.BlockSpec((group, 16, width), one),
                pl.BlockSpec((group, channels, width), one),
                pl.BlockSpec((group, filters * channels, width), one),
            ],
            out_specs=pl.BlockSpec((channels, filters * channels), lambda *_: (0, 0)),
            scratch_shapes=[pltpu.VMEM((blocks, channels, width), F32)],
        ),
        out_shape=jax.ShapeDtypeStruct((channels, filters * channels), F32),
        compiler_params=params,
        cost_estimate=cost(10e9),
        name="atom_grad",
    )(asked_ids, returned, where, message, sums)
    grad_atom, grad_filter, grad_mix, grad_readout = reduce_all(
        (grad_atom, grad_filter, grad_mix, grad_readout), axes, "grad_reduce", 0
    )
    return (density.reshape(tiles, probes), grad_atom, grad_filter, grad_mix, grad_readout[0])


def solution(mesh):
    return jax.shard_map(
        body,
        mesh=mesh,
        in_specs=(
            P(("space", "tile"), None, None),
            P(("space", "tile"), None, None),
            P(("space", "tile")),
            P(("space", "tile"), None),
            P(("space", "tile"), None, None),
            P(("space", "tile"), None),
            P(("space", "tile"), None),
            P(),
            P(),
            P(),
            P(),
        ),
        out_specs=(P(("space", "tile"), None), P(), P(), P(), P()),
        check_vma=False,
    )
```
